256 devices in a mesh: leaf: 8 (over z), row: 2 (over core), col: 16 (over y, x).
Axes of the slice: x: 4, y: 4, z: 8, core: 2. Of those that a mesh axis runs over, the one named last changes fastest.
Arguments:
- front_tiles: bfloat16 [8, 2, 16, 2, 128, 2, 16, 2, 128], P('leaf', None, None, 'row', None, None, 'col'), as said below
- regular: float32 [8, 2, 16, 2, 128], P('leaf', None, 'col', 'row'), may hold values from 0.25 to 2.5
- child_map: int32 [8, 62], P('leaf'), may hold values from 0 to 63, as said below
Outputs:
- panel_factor: float32 [8, 2, 16, 2, 128, 256], P('leaf', None, None, 'row', None, 'col')
- parent_update: float32 [8, 1, 16, 2, 128, 2, 16, 2, 128], P('leaf', None, None, 'row', None, None, 'col')
The draws below stay inside these ranges and needn't reach their ends.
Inputs may be any that keep to these rules, and one draw needn't show every extreme that they name: Each leaf's front_tiles form a symmetric positive semidefinite matrix, the product of a block-sparse constraint matrix (2 of 16 variable blocks per block row), a positive diagonal and its transpose; blocks that share no variable block are zero. `child_map`: within a leaf the entries are strictly increasing.
All inputs are finite; a program needn't handle non-finite values.
Results may differ from the reference program's by a relative error of at most 0.0016.
Values may be sent and summed in bfloat16 or wider, within the bound.
A program may use at most 128 MiB of HBM per device.

```python
import math
import jax
import jax.numpy as jnp
from jax import lax

TILE = 128
NB = 64
NR = 2
VB = 16
LBO = 2
PB = 2
NCB = 62
N_LEAF = 8
N_ROW = 2
N_COL = 16


def draw_front_tiles(key, part):
    order_full = NB * TILE
    value_top = 16
    exp_low = -2
    exp_high = 3
    energy = 85.0
    scale_factor = 1.0 / (energy * NR * TILE)

    def one_front(leaf_key):
        key_ids, key_vals, key_diag = jax.random.split(leaf_key, 3)
        scores = jax.random.randint(key_ids, (NB, VB), 0, 1 << 20) * VB + jnp.arange(VB, dtype=jnp.int32)[None, :]
        chosen_ids = lax.top_k(scores, NR)[1].astype(jnp.int32)
        values = jax.random.randint(key_vals, (NB, NR, TILE, TILE), 1 - value_top, value_top).astype(jnp.float32)
        weights = jnp.exp2(jax.random.randint(key_diag, (VB, TILE), exp_low, exp_high).astype(jnp.float32))
        dense_rows = jnp.zeros((NB, TILE, VB, TILE), jnp.float32)
        dense_rows = dense_rows.at[jnp.arange(NB, dtype=jnp.int32)[:, None], :, chosen_ids, :].set(values)
        scaled = values * weights[chosen_ids][:, :, None, :]

        def one_row(pair_args):
            tiles_row, ids_row = pair_args
            picked = jnp.take(dense_rows, ids_row, axis=2)
            return jnp.einsum('atx,jyax->tjy', tiles_row, picked, precision=lax.Precision.HIGHEST).reshape(TILE, order_full)
        rows_all = lax.map(one_row, (scaled, chosen_ids)).reshape(order_full, order_full)
        return (rows_all * scale_factor).astype(jnp.bfloat16)
    leaf_keys = jax.random.split(jax.random.fold_in(key, 11), N_LEAF)
    fronts = lax.map(one_front, leaf_keys)
    return fronts.reshape(N_LEAF, LBO, N_COL, N_ROW, TILE, LBO, N_COL, N_ROW, TILE)


def draw_child_map(key, part):
    leaf_keys = jax.random.split(jax.random.fold_in(key, 23), N_LEAF)

    def one_map(map_key):
        order = jax.random.permutation(map_key, NB).astype(jnp.int32)
        keep = order < NCB
        ranks = jnp.cumsum(keep.astype(jnp.int32)) - 1
        slots = jnp.where(keep, ranks, NCB).astype(jnp.int32)
        return jnp.zeros((NCB,), jnp.int32).at[slots].set(jnp.arange(NB, dtype=jnp.int32), mode='drop')
    return jax.vmap(one_map)(leaf_keys).astype(jnp.int32)


def level_of(own_key, extent, cuts, least, high):
    factor_of = 1.0
    for axis_at, shards_of in cuts:
        steps = jax.random.uniform(jax.random.fold_in(jax.random.fold_in(own_key, 6), axis_at), (shards_of,), jnp.float32, least / len(cuts), high / len(cuts))
        factor_of = factor_of * jnp.repeat(jnp.exp(steps), extent[axis_at] // shards_of).reshape((-1,) + (1,) * (len(extent) - 1 - axis_at))
    return factor_of


def setup_inputs(seed: int = 0) -> dict:
    streams_of = jax.random.split(jax.random.key(seed), 4)
    front_tiles = draw_front_tiles(jax.random.fold_in(streams_of[3], 71), 0)
    regular = jnp.clip(jnp.exp(math.log(2.5) - 2.3025851 * jax.random.uniform(streams_of[1], (N_LEAF, LBO, N_COL, N_ROW, TILE), jnp.float32) ** level_of(streams_of[1], (N_LEAF, LBO, N_COL, N_ROW, TILE), ((0, 8), (2, 16), (3, 2)), -0.2, 0.2)), 0.25, 2.5)
    child_map = draw_child_map(jax.random.fold_in(streams_of[3], 71), 0)
    return dict(front_tiles=front_tiles, regular=regular, child_map=child_map)


def reference(front_tiles, regular, child_map):
    order_full = NB * TILE
    panel_cols = PB * TILE
    half_outer = LBO // 2
    factors = []
    parents = []
    for pair_id in range(N_LEAF // 2):
        parent_sum = jnp.zeros((NB, TILE, NB, TILE), jnp.float32)
        for leaf_id in (2 * pair_id, 2 * pair_id + 1):
            front_full = front_tiles[leaf_id].reshape(order_full, order_full).astype(jnp.float32)
            front_full = front_full + jnp.diag(regular[leaf_id].reshape(order_full))
            top_factor = jnp.linalg.cholesky(front_full[:panel_cols, :panel_cols])
            lower_rows = jax.scipy.linalg.solve_triangular(top_factor, front_full[panel_cols:, :panel_cols].T, lower=True).T
            factors.append(jnp.concatenate([top_factor, lower_rows], axis=0).reshape(LBO, N_COL, N_ROW, TILE, panel_cols))
            schur_rest = front_full[panel_cols:, panel_cols:] - jnp.dot(lower_rows, lower_rows.T, precision=lax.Precision.HIGHEST)
            rounded = lax.optimization_barrier(schur_rest.astype(jnp.bfloat16)).astype(jnp.float32)
            child_tiles = jnp.transpose(rounded.reshape(NCB, TILE, NCB, TILE), (0, 2, 1, 3))
            targets = child_map[leaf_id].astype(jnp.int32)
            parent_sum = parent_sum.at[targets[:, None], :, targets[None, :], :].add(child_tiles)
        parent_sum = parent_sum.reshape(LBO, N_COL, N_ROW, TILE, LBO, N_COL, N_ROW, TILE)
        parents.append(parent_sum[:half_outer])
        parents.append(parent_sum[half_outer:])
    return (jnp.stack(factors), jnp.stack(parents))
```

```python
import jax
import jax.numpy as jnp
from jax import lax
from jax.experimental import pallas as pl
from jax.experimental.pallas import tpu as pltpu
from jax.sharding import PartitionSpec as P

T = 128
N = 256
COLS = 16
HALF = 16
CHUNK = 4 * T
PACK = CHUNK + 16
HIGHEST = lax.Precision.HIGHEST
F32 = jnp.float32
BF16 = jnp.bfloat16


def dot(a, b, dims, precision=None):
    return lax.dot_general(a, b, (dims, ((), ())), precision=precision, preferred_element_type=F32)


NN = ((1,), (0,))
NT = ((1,), (1,))
TN = ((0,), (0,))


def strip_factor(strip, start):
    lane = lax.broadcasted_iota(jnp.int32, (8, T), 1)
    sub = lax.broadcasted_iota(jnp.int32, (8, T), 0)
    turned = pltpu.roll(strip[:, :T], lax.rem(T - start, T), axis=1)
    a = {}
    for j in range(8):
        column = jnp.broadcast_to(turned[:, j : j + 1], (8, T))
        for i in range(j, 8):
            a[i, j] = jnp.broadcast_to(column[i : i + 1, :], (8, T))
    low, inv = {}, {}
    for k in range(8):
        inv[k, k] = lax.rsqrt(a[k, k])
        for i in range(k + 1, 8):
            low[i, k] = a[i, k] * inv[k, k]
        for j in range(k + 1, 8):
            for i in range(j, 8):
                a[i, j] = a[i, j] - low[i, k] * low[j, k]
    for k in range(8):
        for i in range(k + 1, 8):
            total = low[i, k] * inv[k, k]
            for m in range(k + 1, i):
                total = total + low[i, m] * inv[m, k]
            inv[i, k] = -inv[i, i] * total
    out = None
    for m in range(8):
        weight = jnp.zeros((8, T), F32)
        for k in range(m, 8):
            weight = jnp.where(sub == k, inv[k, m], weight)
        row = jnp.broadcast_to(strip[m : m + 1, :], (8, 2 * T))
        term = jnp.concatenate([weight, weight], axis=1) * row
        out = term if out is None else out + term
    upper = jnp.where(lane >= start + sub, out[:, :T], 0.0)
    later = jnp.where(lane >= start + 8, out[:, :T], 0.0)
    return jnp.concatenate([upper, out[:, T:]], axis=1), later


def eliminate(work):
    def body(b, carry):
        start = pl.multiple_of(b * 8, 8)
        for l in range(2):
            strip, later = strip_factor(work[l, pl.ds(start, 8), :], start)
            update = dot(later, strip, TN, HIGHEST)
            work[l] = work[l] - update
            work[l, pl.ds(start, 8), :] = strip
        return carry

    lax.fori_loop(0, T // 8, body, 0)


def factor_kernel(s_ref, upper_ref, linv_ref, sinv_ref, work, full):
    eye = jnp.where(
        lax.broadcasted_iota(jnp.int32, (T, T), 0) == lax.broadcasted_iota(jnp.int32, (T, T), 1), 1.0, 0.0
    ).astype(F32)
    for l in range(2):
        work[l, :, :T] = s_ref[l, :T, :T]
        work[l, :, T:] = eye
    eliminate(work)
    for l in range(2):
        inverse = work[l, :, T:]
        across = dot(inverse, s_ref[l, :T, T:], NN, HIGHEST)
        if l == 0:
            upper_ref[:T, :T] = work[l, :, :T]
            upper_ref[:T, T:] = across
            upper_ref[T:, :T] = jnp.zeros((T, T), F32)
        full[l, :T, :T] = inverse
        full[l, :T, T:] = jnp.zeros((T, T), F32)
        full[l, T:, :T] = dot(across, inverse, TN, HIGHEST)
        work[l, :, :T] = s_ref[l, T:, T:] - dot(across, across, TN, HIGHEST)
        work[l, :, T:] = eye
    eliminate(work)
    for l in range(2):
        inverse = work[l, :, T:]
        if l == 0:
            upper_ref[T:, T:] = work[l, :, :T]
        full[l, T:, :T] = -dot(inverse, full[l, T:, :T], NN, HIGHEST)
        full[l, T:, T:] = inverse
        whole = full[l]
        square = dot(whole, whole, TN, HIGHEST)
        high = square.astype(BF16)
        sinv_ref[l, 0] = high
        sinv_ref[l, 1] = (square - high.astype(F32)).astype(BF16)
    whole = full[0]
    high = whole.astype(BF16)
    linv_ref[0] = high
    linv_ref[1] = (whole - high.astype(F32)).astype(BF16)


def factor(top):
    return pl.pallas_call(
        factor_kernel,
        name="factor",
        out_shape=(
            jax.ShapeDtypeStruct((N, N), F32),
            jax.ShapeDtypeStruct((2, N, N), BF16),
            jax.ShapeDtypeStruct((2, 2, N, N), BF16),
        ),
        scratch_shapes=[pltpu.VMEM((2, T, 2 * T), F32), pltpu.VMEM((2, N, N), F32)],
        compiler_params=pltpu.CompilerParams(vmem_limit_bytes=24 << 20),
        cost_estimate=pl.CostEstimate(flops=4 * N**3, bytes_accessed=4 << 20, transcendentals=0),
    )(top)


def place_of(q):
    return (q // 2) % COLS, (q // (2 * COLS)) * 2 + q % 2


def cols_kernel(src, at, p_ref, sinv_ref, out_ref):
    rows = jnp.concatenate([p_ref[0, 0, 0], p_ref[1, 0, 0]], axis=1)
    value = dot(sinv_ref[0, 0], rows, NT) + dot(sinv_ref[0, 1], rows, NT)
    high = value.astype(BF16)
    out_ref[0, 0] = high
    out_ref[0, 1] = (value - high.astype(F32)).astype(BF16)


def cols_factor(src, at, gathered, sinv):
    def p_map(l, j, src, at):
        parent = ((j // 2) * COLS + at[1]) * 2 + j % 2
        chip, slot = place_of(src[l * 64 + parent])
        return (0, chip, l, slot, 0)

    return pl.pallas_call(
        cols_kernel,
        name="cols_factor",
        out_shape=jax.ShapeDtypeStruct((2, 2, N, CHUNK), BF16),
        grid_spec=pltpu.PrefetchScalarGridSpec(
            num_scalar_prefetch=2,
            grid=(2, 4),
            in_specs=[
                pl.BlockSpec((2, 1, 1, T, T), p_map),
                pl.BlockSpec((1, 2, N, N), lambda l, j, src, at: (l, 0, 0, 0)),
            ],
            out_specs=pl.BlockSpec((1, 2, N, T), lambda l, j, src, at: (l, 0, 0, j)),
        ),
        cost_estimate=pl.CostEstimate(flops=8 * 4 * N * N * T, bytes_accessed=4 << 20, transcendentals=0),
    )(src, at, gathered, sinv)


def panel_kernel(at, p_ref, linv_ref, upper_ref, out_ref):
    step = pl.program_id(0)
    row, col = at[0], at[1]
    start = pl.multiple_of(col * 16, 16)
    weights = jnp.concatenate([linv_ref[0, pl.ds(start, 16), :], linv_ref[1, pl.ds(start, 16), :]], axis=0)
    for o in range(2):
        offset = pl.multiple_of((o * 2 + row) * T, T)
        rows = jnp.concatenate([p_ref[0, 0, 0, pl.ds(offset, T), :], p_ref[1, 0, 0, pl.ds(offset, T), :]], axis=1)
        both = dot(weights, rows, NT)
        value = both[:16] + both[16:]
        if o == 0:
            first = upper_ref[pl.ds(start, 16), :T]
            second = upper_ref[pl.ds(start, 16), T:]
            value = jnp.where(step == 0, jnp.where(row == 0, first, second), value)
        out_ref[o, 0] = value


def panel_out(at, gathered, linv, upper):
    return pl.pallas_call(
        panel_kernel,
        name="panel_out",
        out_shape=jax.ShapeDtypeStruct((2, COLS, 16, T), F32),
        grid_spec=pltpu.PrefetchScalarGridSpec(
            num_scalar_prefetch=1,
            grid=(COLS,),
            in_specs=[
                pl.BlockSpec((2, 1, 1, CHUNK, T), lambda i, at: (0, i, 0, 0, 0)),
                pl.BlockSpec((2, N, N), lambda i, at: (0, 0, 0)),
                pl.BlockSpec((N, N), lambda i, at: (0, 0)),
            ],
            out_specs=pl.BlockSpec((2, 1, 16, T), lambda i, at: (0, i, 0, 0)),
        ),
        cost_estimate=pl.CostEstimate(flops=4 * 8192 * N * 16, bytes_accessed=6 << 20, transcendentals=0),
    )(at, gathered, linv, upper)


def parent_kernel(src, at, *refs):
    data, (p_own, p_other, w_ref, reg_ref, out_ref, buf) = refs[:8], refs[8:]
    row, col, base, half = at[0], at[1], at[2], at[3]
    parent_row = 2 * (HALF * half + pl.program_id(0)) + row
    diagonal = lax.broadcasted_iota(jnp.int32, (T, T), 0) == lax.broadcasted_iota(jnp.int32, (T, T), 1)
    for l in range(2):
        from_row = src[l * 64 + parent_row]
        mine = from_row % 2 == row

        @pl.when(mine)
        def _():
            buf[:CHUNK] = data[4 * l][0].astype(F32)
            buf[CHUNK:] = data[4 * l + 1][0].astype(F32)

        @pl.when(jnp.logical_not(mine))
        def _():
            buf[:CHUNK] = data[4 * l + 2][0].astype(F32)
            buf[CHUNK:] = data[4 * l + 3][0].astype(F32)

        p_ref = (p_own, p_other)[l]
        rows = jnp.concatenate([p_ref[0, 0, 0], p_ref[1, 0, 0]], axis=1)
        update = dot(rows, w_ref[l, 0], NN) + dot(rows, w_ref[l, 1], NN)
        for j in range(4):
            parent_col = ((j // 2) * COLS + col) * 2 + j % 2
            from_col = src[l * 64 + parent_col]
            chip, slot = place_of(from_col)
            offset = jnp.where(chip == col, 0, CHUNK) + slot
            value = buf[pl.ds(offset, T, stride=4), :]
            gain = jnp.where(from_row == from_col, 1.0, 0.0) * reg_ref[l, pl.ds(from_col, 1), :]
            value = value + jnp.where(diagonal, gain, 0.0)
            value = value - update[:, j * T : (j + 1) * T]
            value = value.astype(BF16).astype(F32)
            there = jnp.logical_and(from_row > 0, from_col > 0)
            value = jnp.where(there, value, 0.0)
            target = (0, pl.ds(j, T, stride=4), slice(None))
            if l == 0:
                out_ref[target] = value
            else:
                out_ref[target] = out_ref[target] + value


def parent_out(src, at, data, gathered, weights, reg):
    def chunk_spec(l, partner):
        def index(i, src, at):
            q = src[l * 64 + 2 * (HALF * at[3] + i) + at[0]]
            wanted = (q % 2 == at[0]) != partner
            return (jnp.where(wanted, jnp.maximum(q // 2 - at[2], 0), 0), 0, 0)

        return pl.BlockSpec((1, CHUNK, T), index)

    def p_spec(l):
        def index(i, src, at):
            chip, slot = place_of(src[l * 64 + 2 * (HALF * at[3] + i) + at[0]])
            return (0, chip, l, slot, 0)

        return pl.BlockSpec((2, 1, 1, T, T), index)

    return pl.pallas_call(
        parent_kernel,
        name="parent_out",
        out_shape=jax.ShapeDtypeStruct((HALF, CHUNK, T), F32),
        grid_spec=pltpu.PrefetchScalarGridSpec(
            num_scalar_prefetch=2,
            grid=(HALF,),
            in_specs=[chunk_spec(l, p) for l in range(2) for p in (False, True) for _ in range(2)]
            + [
                p_spec(0),
                p_spec(1),
                pl.BlockSpec((2, 2, N, CHUNK), lambda i, src, at: (0, 0, 0, 0)),
                pl.BlockSpec((2, 64, T), lambda i, src, at: (0, 0, 0)),
            ],
            out_specs=pl.BlockSpec((1, CHUNK, T), lambda i, src, at: (i, 0, 0)),
            scratch_shapes=[pltpu.VMEM((2 * CHUNK, T), F32)],
        ),
        compiler_params=pltpu.CompilerParams(vmem_limit_bytes=32 << 20),
        cost_estimate=pl.CostEstimate(flops=2 * 2 * 4096 * N * CHUNK, bytes_accessed=14 << 20, transcendentals=0),
    )(src, at, *data, gathered, gathered, weights, reg)


def turned(value, axis, length, by):
    return lax.ppermute(value, axis, [(i, (i + by) % length) for i in range(length)])


def swapped(value, axis, length):
    return lax.ppermute(value, axis, [(i, i ^ 1) for i in range(length)])


def shards(front_tiles, regular, child_map):
    leaves = lax.axis_size("leaf")
    row, col = lax.axis_index("row"), lax.axis_index("col")
    half = lax.axis_index("leaf") % 2
    base = jnp.where(half == 0, 1, HALF)
    tiles = front_tiles.reshape(2 * COLS, CHUNK, T)

    columns = tiles[0].reshape(T, 4, T).transpose(1, 2, 0).reshape(CHUNK, T)
    gains = regular.reshape(2, T)
    high = lax.reduce_precision(gains, 8, 7)
    rest = gains - high
    middle = lax.reduce_precision(rest, 8, 7)
    pieces = jnp.concatenate([high, middle, rest - middle], axis=0).astype(BF16)
    parents = jnp.arange(64, dtype=jnp.int32)
    match = child_map.reshape(1, -1) == parents[:, None]
    source = jnp.sum(jnp.where(match, 2 + jnp.arange(62, dtype=jnp.int32)[None, :], 0), axis=1)
    source = jnp.pad(source, (0, T - 64)).astype(BF16)[None]
    pack = jnp.concatenate([columns, pieces, source, jnp.zeros((9, T), BF16)], axis=0)
    packs = jnp.stack([pack, swapped(pack, "leaf", leaves)])
    gathered = lax.all_gather(packs, ("row", "col"), axis=0, tiled=False)
    gathered = gathered.reshape(2, COLS, 2, PACK, T)

    keep = lax.dynamic_slice_in_dim(tiles, base, HALF, 0)
    send = lax.dynamic_slice_in_dim(tiles, HALF + 1 - base, HALF, 0)
    other = swapped(send, "leaf", leaves)
    keep_next = turned(keep, "col", COLS, -1)
    other_next = turned(other, "col", COLS, -1)
    data = [keep, keep_next, swapped(keep, "row", 2), swapped(keep_next, "row", 2)]
    data += [other, other_next, swapped(other, "row", 2), swapped(other_next, "row", 2)]

    pieces = gathered[:, :, :, CHUNK : CHUNK + 6].astype(F32).reshape(2, COLS, 2, 3, 2, T)
    reg = (pieces[:, :, :, 0] + pieces[:, :, :, 1]) + pieces[:, :, :, 2]
    reg = reg.transpose(2, 3, 1, 0, 4).reshape(2, 64, T)
    src = gathered[0, 0, :, CHUNK + 6, :64].astype(jnp.int32).reshape(-1)
    top = gathered[:, 0, :, :N].transpose(1, 2, 0, 3).reshape(2, N, N).astype(F32)
    top = top + jnp.where(jnp.eye(N, dtype=jnp.bool_)[None], reg[:, :2].reshape(2, 1, N), 0.0)
    at = jnp.stack([row, col, base, half]).astype(jnp.int32)

    upper, linv, sinv = factor(top)
    weights = cols_factor(src, at, gathered, sinv)
    panel = panel_out(at, gathered, linv, upper)
    panel = panel.transpose(0, 1, 3, 2).reshape(1, 2, COLS, 1, T, 16)
    parent = parent_out(src, at, data, gathered, weights, reg)
    return panel, parent.reshape(1, 1, COLS, 1, T, 2, 1, 2, T)


def solution(mesh):
    return jax.shard_map(
        shards,
        mesh=mesh,
        in_specs=(
            P("leaf", None, None, "row", None, None, "col", None, None),
            P("leaf", None, "col", "row", None),
            P("leaf", None),
        ),
        out_specs=(
            P("leaf", None, None, "row", None, "col"),
            P("leaf", None, None, "row", None, None, "col", None, None),
        ),
        check_vma=False,
    )
```

```python
import jax
import jax.numpy as jnp
from jax import lax
from jax.experimental import pallas as pl
from jax.experimental.pallas import tpu as pltpu
from jax.sharding import PartitionSpec as P

T = 128
N = 256
COLS = 16
HALF = 16
CHUNK = 4 * T
PACK = CHUNK + 16
HIGHEST = lax.Precision.HIGHEST
F32 = jnp.float32
BF16 = jnp.bfloat16


def dot(a, b, dims, precision=None):
    return lax.dot_general(a, b, (dims, ((), ())), precision=precision, preferred_element_type=F32)


NN = ((1,), (0,))
NT = ((1,), (1,))
TN = ((0,), (0,))


def strip_factor(strip, start):
    lane = lax.broadcasted_iota(jnp.int32, (8, T), 1)
    sub = lax.broadcasted_iota(jnp.int32, (8, T), 0)
    turned = pltpu.roll(strip[:, :T], lax.rem(T - start, T), axis=1)
    a = {}
    for j in range(8):
        column = jnp.broadcast_to(turned[:, j : j + 1], (8, T))
        for i in range(j, 8):
            a[i, j] = jnp.broadcast_to(column[i : i + 1, :], (8, T))
    low, inv = {}, {}
    for k in range(8):
        inv[k, k] = lax.rsqrt(a[k, k])
        for i in range(k + 1, 8):
            low[i, k] = a[i, k] * inv[k, k]
        for j in range(k + 1, 8):
            for i in range(j, 8):
                a[i, j] = a[i, j] - low[i, k] * low[j, k]
    for k in range(8):
        for i in range(k + 1, 8):
            total = low[i, k] * inv[k, k]
            for m in range(k + 1, i):
                total = total + low[i, m] * inv[m, k]
            inv[i, k] = -inv[i, i] * total
    out = None
    for m in range(8):
        weight = jnp.zeros((8, T), F32)
        for k in range(m, 8):
            weight = jnp.where(sub == k, inv[k, m], weight)
        row = jnp.broadcast_to(strip[m : m + 1, :], (8, 2 * T))
        term = jnp.concatenate([weight, weight], axis=1) * row
        out = term if out is None else out + term
    upper = jnp.where(lane >= start + sub, out[:, :T], 0.0)
    later = jnp.where(lane >= start + 8, out[:, :T], 0.0)
    return jnp.concatenate([upper, out[:, T:]], axis=1), later


def split(value):
    high = value.astype(BF16)
    return high, (value - high.astype(F32)).astype(BF16)


def eliminate(work):
    def body(b, carry):
        start = pl.multiple_of(b * 8, 8)
        for l in range(2):
            strip, later = strip_factor(work[l, pl.ds(start, 8), :], start)
            high, low = split(strip)
            later_high, later_low = split(later)
            left = jnp.concatenate([later_high.astype(F32), later_high.astype(F32), later_low.astype(F32)], axis=0)
            right = jnp.concatenate([high.astype(F32), low.astype(F32), high.astype(F32)], axis=0)
            work[l] = work[l] - dot(left.astype(BF16), right.astype(BF16), TN)
            work[l, pl.ds(start, 8), :] = strip
        return carry

    lax.fori_loop(0, T // 8, body, 0)


def factor(top, work, full, upper, linv, sinv, between):
    eye = lax.broadcasted_iota(jnp.int32, (T, T), 0) == lax.broadcasted_iota(jnp.int32, (T, T), 1)
    one = jnp.where(eye, 1.0, 0.0).astype(F32)

    def block(q, s, l):
        value = top[s, l, q * T : (q + 1) * T, :].astype(F32)
        if q == s:
            parts = top[s, l, CHUNK : CHUNK + 16, :].astype(F32)
            gain = (parts[0:1] + parts[2:3]) + parts[4:5]
            value = value + jnp.where(eye, gain, 0.0)
        return value

    for l in range(2):
        work[l, :, :T] = block(0, 0, l)
        work[l, :, T:] = one
    eliminate(work)
    between()
    for l in range(2):
        inverse = work[l, :, T:]
        across = dot(inverse, block(0, 1, l), NN, HIGHEST)
        if l == 0:
            upper[:, :T] = jnp.concatenate([work[l, :, :T], jnp.zeros((T, T), F32)], axis=0)
            upper[:T, T:] = across
        full[l, :T, :T] = inverse
        full[l, :T, T:] = jnp.zeros((T, T), F32)
        full[l, T:, :T] = dot(across, inverse, TN, HIGHEST)
        work[l, :, :T] = block(1, 1, l) - dot(across, across, TN, HIGHEST)
        work[l, :, T:] = one
    eliminate(work)
    for l in range(2):
        inverse = work[l, :, T:]
        if l == 0:
            upper[T:, T:] = work[l, :, :T]
        full[l, T:, :T] = -dot(inverse, full[l, T:, :T], NN, HIGHEST)
        full[l, T:, T:] = inverse
        whole = full[l]
        sinv[l, 0], sinv[l, 1] = split(dot(whole, whole, TN, HIGHEST))
    linv[0], linv[1] = split(full[0])


PARTS = 4
ROWS = HALF // PARTS
MESH = pl.DeviceIdType.MESH


def exchange_kernel(
    tiles, pack, kn, oth, on, kx, knx, ox, onx, spread, panel, sinv, reg,
    top, own, gains, work, full, upper, linv,
    local_sem, z_sem, x_sem, y_sem, core_sem, bulk_sem, pass_sem,
):
    leaf, row, col = lax.axis_index("leaf"), lax.axis_index("row"), lax.axis_index("col")
    y, x = col // 4, col % 4
    sibling = leaf + 1 - 2 * (leaf % 2)
    before, after = lax.rem(col + COLS - 1, COLS), lax.rem(col + 1, COLS)
    half = leaf % 2
    keep = 1 + half * (HALF - 1)
    send = HALF - half * (HALF - 1)
    here = (leaf, row, col)
    across = (leaf, 1 - row, col)
    x_peer = [(leaf, row, y * 4 + lax.rem(x + d, 4)) for d in (1, 2, 3)]
    y_peer = [(leaf, row, lax.rem(y + d, 4) * 4 + x) for d in (1, 2, 3)]

    peers = [(sibling, row, col), (sibling, row, before), (sibling, row, after)]
    peers += [(leaf, row, before), (leaf, row, after), across] + x_peer + y_peer
    barrier = pltpu.get_barrier_semaphore()
    for peer in peers:
        pl.semaphore_signal(barrier, inc=1, device_id=peer, device_id_type=MESH)
    pl.semaphore_wait(barrier, len(peers))

    def remote(source, target, sems, peer):
        return pltpu.make_async_remote_copy(
            src_ref=source, dst_ref=target, send_sem=sems.at[0], recv_sem=sems.at[1],
            device_id=peer, device_id_type=MESH,
        )

    sent = []

    def start(copy):
        copy.start()
        sent.append(copy)
        return copy

    to_sibling = start(remote(pack, spread.at[row, y, x, 1], z_sem, (sibling, row, col)))
    x_copies = [start(remote(pack, spread.at[row, y, x, 0], x_sem.at[0, d], x_peer[d])) for d in range(3)]
    place = pltpu.make_async_copy(pack, spread.at[row, y, x, 0], local_sem.at[0])
    place.start()
    to_sibling.wait_recv()
    x_copies += [
        start(remote(spread.at[row, y, x, 1], spread.at[row, y, x, 1], x_sem.at[1, d], x_peer[d])) for d in range(3)
    ]

    bulk = []
    for k in range(PARTS):
        kept, gone = tiles.at[pl.ds(keep + k * ROWS, ROWS)], tiles.at[pl.ds(send + k * ROWS, ROWS)]
        part = pl.ds(k * ROWS, ROWS)
        bulk.append([
            start(remote(kept, kn.at[part], bulk_sem.at[0, k], (leaf, row, before))),
            start(remote(gone, oth.at[part], bulk_sem.at[1, k], (sibling, row, col))),
            start(remote(gone, on.at[part], bulk_sem.at[2, k], (sibling, row, before))),
            start(remote(kept, kx.at[part], bulk_sem.at[3, k], across)),
        ])

    place.wait()
    for copy in x_copies:
        copy.wait_recv()
    y_copies = [
        [start(remote(spread.at[row, y, g], spread.at[row, y, g], y_sem.at[g, d], y_peer[d])) for d in range(3)]
        for g in range(4)
    ]

    core_copies = []

    def over_core(g):
        for copy in y_copies[g]:
            copy.wait_recv()
        core_copies.append(start(remote(spread.at[row, :, g], spread.at[row, :, g], core_sem.at[g], across)))

    over_core(0)
    core_copies[0].wait_recv()
    loads = [pltpu.make_async_copy(spread.at[s, 0, 0], top.at[s], local_sem.at[1 + s]) for s in range(2)]
    for load in loads:
        load.start()
    for load in loads:
        load.wait()

    def between():
        over_core(1)
        over_core(2)

    factor(top, work, full, upper, linv, sinv, between)
    over_core(3)
    for copy in core_copies[1:]:
        copy.wait_recv()
    loads = [pltpu.make_async_copy(spread.at[:, :, :, 0, pl.ds(0, CHUNK)], own, local_sem.at[3])]
    loads += [pltpu.make_async_copy(spread.at[:, :, :, :, pl.ds(CHUNK, 16)], gains, local_sem.at[4])]
    for load in loads:
        load.start()
    for load in loads:
        load.wait()

    first = pl.multiple_of(col * 16, 16)
    weights = jnp.concatenate([linv[0, pl.ds(first, 16), :], linv[1, pl.ds(first, 16), :]], axis=0)

    def chip(at, carry):
        ay, ax = at // 4, at % 4
        for o in range(2):
            span = pl.ds(pl.multiple_of((o * 2 + row) * T, T), T)
            rows = jnp.concatenate([own[0, ay, ax, span, :], own[1, ay, ax, span, :]], axis=1)
            both = dot(weights, rows, NT)
            panel[o, at] = both[:16] + both[16:]
        for s in range(2):
            for l in range(2):
                parts = gains[s, ay, ax, l].astype(F32)
                for o in range(2):
                    gain = (parts[o : o + 1] + parts[2 + o : 3 + o]) + parts[4 + o : 5 + o]
                    reg[l, pl.ds((o * COLS + at) * 2 + s, 1), :] = gain
        return carry

    lax.fori_loop(0, COLS, chip, 0)
    panel[0, 0] = upper[pl.ds(first, 16), pl.ds(pl.multiple_of(row * T, T), T)]

    passed = []
    for k in range(PARTS):
        part = pl.ds(k * ROWS, ROWS)
        for n, (source, target) in enumerate(((kn, knx), (oth, ox), (on, onx))):
            bulk[k][n].wait_recv()
            passed.append(start(remote(source.at[part], target.at[part], pass_sem.at[n, k], across)))
    for k in range(PARTS):
        bulk[k][3].wait_recv()
    for copy in passed:
        copy.wait_recv()
    for copy in sent:
        copy.wait_send()


def exchange(tiles, pack):
    big = jax.ShapeDtypeStruct((HALF, CHUNK, T), BF16)
    spread = jax.ShapeDtypeStruct((2, 4, 4, 2, PACK, T), BF16)
    dma = pltpu.SemaphoreType.DMA
    anywhere, vmem = pl.BlockSpec(memory_space=pl.ANY), pl.BlockSpec(memory_space=pltpu.VMEM)
    return pl.pallas_call(
        exchange_kernel,
        name="exchange",
        out_shape=(big,) * 7 + (
            spread,
            jax.ShapeDtypeStruct((2, COLS, 16, T), F32),
            jax.ShapeDtypeStruct((2, 2, N, N), BF16),
            jax.ShapeDtypeStruct((2, 64, T), F32),
        ),
        in_specs=[anywhere, anywhere],
        out_specs=(anywhere,) * 8 + (vmem,) * 3,
        scratch_shapes=[
            pltpu.VMEM((2, 2, PACK, T), BF16),
            pltpu.VMEM((2, 4, 4, CHUNK, T), BF16),
            pltpu.VMEM((2, 4, 4, 2, 16, T), BF16),
            pltpu.VMEM((2, T, 2 * T), F32),
            pltpu.VMEM((2, N, N), F32),
            pltpu.VMEM((N, N), F32),
            pltpu.VMEM((2, N, N), BF16),
            dma((5,)), dma((2,)), dma((2, 3, 2)), dma((4, 3, 2)), dma((4, 2)), dma((4, PARTS, 2)), dma((3, PARTS, 2)),
        ],
        compiler_params=pltpu.CompilerParams(collective_id=0, has_side_effects=True, vmem_limit_bytes=40 << 20),
        cost_estimate=pl.CostEstimate(flops=4 * N**3, bytes_accessed=40 << 20, transcendentals=0),
    )(tiles, pack)


def place_of(q):
    return (q // 2) % COLS, (q // (2 * COLS)) * 2 + q % 2


def cols_kernel(src, at, p_ref, sinv_ref, out_ref):
    rows = jnp.concatenate([p_ref[0, 0, 0], p_ref[1, 0, 0]], axis=1)
    value = dot(sinv_ref[0, 0], rows, NT) + dot(sinv_ref[0, 1], rows, NT)
    high = value.astype(BF16)
    out_ref[0, 0] = high
    out_ref[0, 1] = (value - high.astype(F32)).astype(BF16)


def cols_factor(src, at, gathered, sinv):
    def p_map(l, j, src, at):
        parent = ((j // 2) * COLS + at[1]) * 2 + j % 2
        chip, slot = place_of(src[l * 64 + parent])
        return (0, chip, l, slot, 0)

    return pl.pallas_call(
        cols_kernel,
        name="cols_factor",
        out_shape=jax.ShapeDtypeStruct((2, 2, N, CHUNK), BF16),
        grid_spec=pltpu.PrefetchScalarGridSpec(
            num_scalar_prefetch=2,
            grid=(2, 4),
            in_specs=[
                pl.BlockSpec((2, 1, 1, T, T), p_map),
                pl.BlockSpec((1, 2, N, N), lambda l, j, src, at: (l, 0, 0, 0)),
            ],
            out_specs=pl.BlockSpec((1, 2, N, T), lambda l, j, src, at: (l, 0, 0, j)),
        ),
        cost_estimate=pl.CostEstimate(flops=8 * 4 * N * N * T, bytes_accessed=4 << 20, transcendentals=0),
    )(src, at, gathered, sinv)


def parent_kernel(src, at, *refs):
    data, (p_own, p_other, w_ref, reg_ref, out_ref, buf) = refs[:8], refs[8:]
    row, col, base, half = at[0], at[1], at[2], at[3]
    parent_row = 2 * (HALF * half + pl.program_id(0)) + row
    diagonal = lax.broadcasted_iota(jnp.int32, (T, T), 0) == lax.broadcasted_iota(jnp.int32, (T, T), 1)
    updates, from_rows = [], []
    for l in range(2):
        from_row = src[l * 64 + parent_row]
        from_rows.append(from_row)
        mine = from_row % 2 == row

        @pl.when(mine)
        def _():
            buf[l, :CHUNK] = data[4 * l][0].astype(F32)
            buf[l, CHUNK:] = data[4 * l + 1][0].astype(F32)

        @pl.when(jnp.logical_not(mine))
        def _():
            buf[l, :CHUNK] = data[4 * l + 2][0].astype(F32)
            buf[l, CHUNK:] = data[4 * l + 3][0].astype(F32)

        p_ref = (p_own, p_other)[l]
        rows = jnp.concatenate([p_ref[0, 0, 0], p_ref[1, 0, 0]], axis=1)
        updates.append(dot(rows, w_ref[l, 0], NN) + dot(rows, w_ref[l, 1], NN))
    for j in range(4):
        total = None
        for l in range(2):
            from_row = from_rows[l]
            from_col = src[l * 64 + ((j // 2) * COLS + col) * 2 + j % 2]
            chip, slot = place_of(from_col)
            span = pl.ds(jnp.where(chip == col, 0, CHUNK) + slot, T, stride=4)

            @pl.when(from_row == from_col)
            def _():
                buf[l, span, :] = buf[l, span, :] + jnp.where(diagonal, reg_ref[l, pl.ds(from_col, 1), :], 0.0)

            value = buf[l, span, :] - updates[l][:, j * T : (j + 1) * T]
            value = value.astype(BF16).astype(F32)
            value = jnp.where(jnp.logical_and(from_row > 0, from_col > 0), value, 0.0)
            total = value if total is None else total + value
        out_ref[0, pl.ds(j, T, stride=4), :] = total


def parent_out(src, at, data, gathered, weights, reg):
    def chunk_spec(l, partner, following):
        def index(i, src, at):
            q = src[l * 64 + 2 * (HALF * at[3] + i) + at[0]]
            wanted = (q % 2 == at[0]) != partner
            less = 0 if l == 0 and not partner and not following else at[2]
            return (jnp.where(wanted, jnp.maximum(q // 2 - less, 0), 0), 0, 0)

        return pl.BlockSpec((1, CHUNK, T), index)

    def p_spec(l):
        def index(i, src, at):
            chip, slot = place_of(src[l * 64 + 2 * (HALF * at[3] + i) + at[0]])
            return (0, chip, l, slot, 0)

        return pl.BlockSpec((2, 1, 1, T, T), index)

    return pl.pallas_call(
        parent_kernel,
        name="parent_out",
        out_shape=jax.ShapeDtypeStruct((HALF, CHUNK, T), F32),
        grid_spec=pltpu.PrefetchScalarGridSpec(
            num_scalar_prefetch=2,
            grid=(HALF,),
            in_specs=[chunk_spec(l, p, f) for l in range(2) for p in (False, True) for f in (False, True)]
            + [
                p_spec(0),
                p_spec(1),
                pl.BlockSpec((2, 2, N, CHUNK), lambda i, src, at: (0, 0, 0, 0)),
                pl.BlockSpec((2, 64, T), lambda i, src, at: (0, 0, 0)),
            ],
            out_specs=pl.BlockSpec((1, CHUNK, T), lambda i, src, at: (i, 0, 0)),
            scratch_shapes=[pltpu.VMEM((2, 2 * CHUNK, T), F32)],
        ),
        compiler_params=pltpu.CompilerParams(vmem_limit_bytes=32 << 20),
        cost_estimate=pl.CostEstimate(flops=2 * 2 * 4096 * N * CHUNK, bytes_accessed=14 << 20, transcendentals=0),
    )(src, at, *data, gathered, gathered, weights, reg)


def shards(front_tiles, regular, child_map):
    row, col = lax.axis_index("row"), lax.axis_index("col")
    half = lax.axis_index("leaf") % 2
    base = jnp.where(half == 0, 1, HALF)
    tiles = front_tiles.reshape(2 * COLS, CHUNK, T)

    columns = tiles[0].reshape(T, 4, T).transpose(1, 2, 0).reshape(CHUNK, T)
    gains = regular.reshape(2, T)
    high = lax.reduce_precision(gains, 8, 7)
    rest = gains - high
    middle = lax.reduce_precision(rest, 8, 7)
    pieces = jnp.concatenate([high, middle, rest - middle], axis=0).astype(BF16)
    parents = jnp.arange(64, dtype=jnp.int32)
    match = child_map.reshape(1, -1) == parents[:, None]
    source = jnp.sum(jnp.where(match, 2 + jnp.arange(62, dtype=jnp.int32)[None, :], 0), axis=1)
    source = jnp.pad(source, (0, T - 64)).astype(BF16)[None]
    pack = jnp.concatenate([columns, pieces, source, jnp.zeros((9, T), BF16)], axis=0)
    kn, oth, on, kx, knx, ox, onx, spread, panel, sinv, reg = exchange(tiles, pack)
    gathered = spread.reshape(2, COLS, 2, PACK, T)
    data = [tiles, kn, kx, knx, oth, on, ox, onx]
    src = gathered[0, 0, :, CHUNK + 6, :64].astype(jnp.int32).reshape(-1)
    at = jnp.stack([row, col, base, half]).astype(jnp.int32)

    weights = cols_factor(src, at, gathered, sinv)
    panel = panel.transpose(0, 1, 3, 2).reshape(1, 2, COLS, 1, T, 16)
    parent = parent_out(src, at, data, gathered, weights, reg)
    return panel, parent.reshape(1, 1, COLS, 1, T, 2, 1, 2, T)


def solution(mesh):
    return jax.shard_map(
        shards,
        mesh=mesh,
        in_specs=(
            P("leaf", None, None, "row", None, None, "col", None, None),
            P("leaf", None, "col", "row", None),
            P("leaf", None),
        ),
        out_specs=(
            P("leaf", None, None, "row", None, "col"),
            P("leaf", None, None, "row", None, None, "col", None, None),
        ),
        check_vma=False,
    )
```

```python
import jax
import jax.numpy as jnp
from jax import lax
from jax.experimental import pallas as pl
from jax.experimental.pallas import tpu as pltpu
from jax.sharding import PartitionSpec as P

T = 128
N = 256
COLS = 16
HALF = 16
CHUNK = 4 * T
BLOCK = 16
PACK = CHUNK + 16
HIGHEST = lax.Precision.HIGHEST
F32 = jnp.float32
BF16 = jnp.bfloat16


def dot(a, b, dims, precision=None):
    return lax.dot_general(a, b, (dims, ((), ())), precision=precision, preferred_element_type=F32)


NN = ((1,), (0,))
NT = ((1,), (1,))
TN = ((0,), (0,))


def unit_inverse(group, lane):
    a = {}
    for j in range(8):
        column = jnp.broadcast_to(group[:, lane + j : lane + j + 1], (8, T))
        for i in range(j, 8):
            a[i, j] = jnp.broadcast_to(column[i : i + 1, :], (8, T))
    low, inv = {}, {}
    for k in range(8):
        inv[k, k] = lax.rsqrt(a[k, k])
        for i in range(k + 1, 8):
            low[i, k] = a[i, k] * inv[k, k]
        for j in range(k + 1, 8):
            for i in range(j, 8):
                a[i, j] = a[i, j] - low[i, k] * low[j, k]
    for k in range(8):
        for i in range(k + 1, 8):
            total = low[i, k] * inv[k, k]
            for m in range(k + 1, i):
                total = total + low[i, m] * inv[m, k]
            inv[i, k] = -inv[i, i] * total
    return inv


def combined(weights, group):
    out = None
    for m in range(8):
        term = weights[m] * jnp.broadcast_to(group[m : m + 1, :], (8, T))
        out = term if out is None else out + term
    return out


def block_factor(rows, start):
    sub = lax.broadcasted_iota(jnp.int32, (8, T), 0)
    moved = pltpu.roll(rows[:, :T], lax.rem(T - start, T), axis=1)
    count = BLOCK // 8
    left = [moved[8 * g : 8 * g + 8] for g in range(count)]
    right = [rows[8 * g : 8 * g + 8, T:] for g in range(count)]
    for b in range(count):
        inv = unit_inverse(left[b], 8 * b)
        weights = []
        for m in range(8):
            weight = jnp.zeros((8, T), F32)
            for k in range(m, 8):
                weight = jnp.where(sub == k, inv[k, m], weight)
            weights.append(weight)
        left_next, right_next = combined(weights, left[b]), combined(weights, right[b])
        for g in range(b + 1, count):
            columns = [jnp.broadcast_to(left[g][:, 8 * b + k : 8 * b + k + 1], (8, T)) for k in range(8)]
            lows = []
            for m in range(8):
                low = columns[0] * inv[m, 0]
                for k in range(1, m + 1):
                    low = low + columns[k] * inv[m, k]
                lows.append(low)
            left[g] = left[g] - combined(lows, left_next)
            right[g] = right[g] - combined(lows, right_next)
        left[b], right[b] = left_next, right_next
    upper = pltpu.roll(jnp.concatenate(left, axis=0), start, axis=1)
    lane = lax.broadcasted_iota(jnp.int32, (BLOCK, T), 1)
    upper = jnp.where(lane >= start + lax.broadcasted_iota(jnp.int32, (BLOCK, T), 0), upper, 0.0)
    later = jnp.where(lane >= start + BLOCK, upper, 0.0)
    return jnp.concatenate([upper, jnp.concatenate(right, axis=0)], axis=1), later


def split(value):
    high = value.astype(BF16)
    return high, (value - high.astype(F32)).astype(BF16)


def eliminate(work, hooks):
    def body(b, carry):
        start = pl.multiple_of(b * BLOCK, BLOCK)
        done = [block_factor(work[l, pl.ds(start, BLOCK), :], start) for l in range(2)]
        for l in range(2):
            rows, later = done[l]
            high, low = split(rows)
            later_high, later_low = split(later)
            left = jnp.concatenate([later_high, later_high, later_low], axis=0)
            right = jnp.concatenate([high, low, high], axis=0)
            work[l] = work[l] - dot(left, right, TN)
            work[l, pl.ds(start, BLOCK), :] = rows
        return carry

    count, steps = len(hooks), T // BLOCK
    for n, hook in enumerate(hooks):
        lax.fori_loop(n * steps // count, (n + 1) * steps // count, body, 0)
        hook()


def factor(top, work, full, upper, linv, sinv, hooks):
    eye = lax.broadcasted_iota(jnp.int32, (T, T), 0) == lax.broadcasted_iota(jnp.int32, (T, T), 1)
    one = jnp.where(eye, 1.0, 0.0).astype(F32)

    def block(q, s, l):
        value = top[s, l, q * T : (q + 1) * T, :].astype(F32)
        if q == s:
            parts = top[s, l, N : N + 16, :].astype(F32)
            gain = (parts[0:1] + parts[2:3]) + parts[4:5]
            value = value + jnp.where(eye, gain, 0.0)
        return value

    for l in range(2):
        work[l, :, :T] = block(0, 0, l)
        work[l, :, T:] = one
    eliminate(work, hooks[0])
    for l in range(2):
        inverse = work[l, :, T:]
        across = dot(inverse, block(0, 1, l), NN, HIGHEST)
        if l == 0:
            upper[:, :T] = jnp.concatenate([work[l, :, :T], jnp.zeros((T, T), F32)], axis=0)
            upper[:T, T:] = across
        full[l, :T, :T] = inverse
        full[l, :T, T:] = jnp.zeros((T, T), F32)
        full[l, T:, :T] = dot(across, inverse, TN, HIGHEST)
        work[l, :, :T] = block(1, 1, l) - dot(across, across, TN, HIGHEST)
        work[l, :, T:] = one
    eliminate(work, hooks[1])
    for l in range(2):
        inverse = work[l, :, T:]
        if l == 0:
            upper[T:, T:] = work[l, :, :T]
        full[l, T:, :T] = -dot(inverse, full[l, T:, :T], NN, HIGHEST)
        full[l, T:, T:] = inverse
        whole = full[l]
        sinv[l, 0], sinv[l, 1] = split(dot(whole, whole, TN, HIGHEST))
    linv[0], linv[1] = split(full[0])


PARTS = 4
FORWARDED = 1
ROWS = HALF // PARTS
MESH = pl.DeviceIdType.MESH


def exchange_kernel(
    tiles, regular, cmap, kn, oth, on, kx, knx, ox, onx, spread, panel, weights, reg,
    pack, raw, wide, top, own, cand, gains, work, full, upper, linv, sinv,
    local_sem, z_sem, lane_sem, lane_core_sem, ring_sem, core_sem, bulk_sem, pass_sem,
):
    leaf, row, col = lax.axis_index("leaf"), lax.axis_index("row"), lax.axis_index("col")
    y, x = col // 4, col % 4
    sibling = leaf + 1 - 2 * (leaf % 2)
    before, after = lax.rem(col + COLS - 1, COLS), lax.rem(col + 1, COLS)
    half = leaf % 2
    keep = 1 + half * (HALF - 1)
    send = HALF - half * (HALF - 1)
    across = (leaf, 1 - row, col)
    x_next = (leaf, row, y * 4 + lax.rem(x + 1, 4))
    y_next = (leaf, row, lax.rem(y + 1, 4) * 4 + x)

    peers = [(sibling, row, col), (sibling, row, before), (sibling, row, after)]
    peers += [(leaf, row, before), (leaf, row, after), across]
    peers += [(leaf, row, y * 4 + lax.rem(x + d, 4)) for d in (1, 3)]
    peers += [(leaf, row, lax.rem(y + d, 4) * 4 + x) for d in (1, 3)]
    first_rows = pltpu.make_async_copy(tiles.at[0], raw, local_sem.at[0])
    first_rows.start()
    barrier = pltpu.get_barrier_semaphore()
    for peer in peers:
        pl.semaphore_signal(barrier, inc=1, device_id=peer, device_id_type=MESH)
    pl.semaphore_wait(barrier, len(peers))

    def remote(source, target, sems, peer):
        return pltpu.make_async_remote_copy(
            src_ref=source, dst_ref=target, send_sem=sems.at[0], recv_sem=sems.at[1],
            device_id=peer, device_id_type=MESH,
        )

    sent = []

    def start(copy):
        copy.start()
        sent.append(copy)
        return copy

    def hop(stage, step):
        l = stage % 2
        along_x = (stage // 2) == l
        origin = lax.rem((x if along_x else y) + 4 - step, 4)
        if stage < 2:
            place = spread.at[row, y, origin, l] if along_x else spread.at[row, origin, x, l]
        else:
            place = spread.at[row, :, origin, l] if along_x else spread.at[row, origin, :, l]
        source = pack if stage == 0 and step == 0 else place
        return start(remote(source, place, ring_sem.at[stage, step], x_next if along_x else y_next))

    bulk = []
    for k in range(PARTS):
        kept, part = tiles.at[pl.ds(keep + k * ROWS, ROWS)], pl.ds(k * ROWS, ROWS)
        bulk.append([
            start(remote(kept, kn.at[part], bulk_sem.at[0, k], (leaf, row, before))),
            start(remote(kept, kx.at[part], bulk_sem.at[3, k], across)),
        ])

    first_rows.wait()
    wide[...] = raw[...].astype(F32)
    for j in range(4):
        pack[j * T : (j + 1) * T, :] = wide[pl.ds(j, T, stride=4), :].T.astype(BF16)
    value = regular[...]
    high = value.astype(BF16).astype(F32)
    rest = value - high
    middle = rest.astype(BF16).astype(F32)
    lane = lax.broadcasted_iota(jnp.int32, (T, T), 1)
    match = cmap[...] == lax.broadcasted_iota(jnp.int32, (T, T), 0)
    source = jnp.where(match, lane + 2, 0).astype(F32).T
    source = jnp.sum(source, axis=0, keepdims=True)
    pack[CHUNK:, :] = jnp.concatenate([high, middle, rest - middle, source, jnp.zeros((9, T), F32)], axis=0).astype(BF16)

    to_sibling = start(remote(pack, spread.at[row, y, x, 1], z_sem, (sibling, row, col)))
    last = [hop(0, 0), None]
    place = pltpu.make_async_copy(pack, spread.at[row, y, x, 0], local_sem.at[0])
    place.start()
    for k in range(PARTS):
        gone, part = tiles.at[pl.ds(send + k * ROWS, ROWS)], pl.ds(k * ROWS, ROWS)
        bulk[k].insert(1, start(remote(gone, oth.at[part], bulk_sem.at[1, k], (sibling, row, col))))
        if k >= FORWARDED:
            bulk[k].insert(2, start(remote(gone, on.at[part], bulk_sem.at[2, k], (sibling, row, before))))

    def forward():
        for k in range(FORWARDED):
            part = pl.ds(k * ROWS, ROWS)
            bulk[k][1].wait_recv()
            bulk[k].insert(2, start(remote(oth.at[part], on.at[part], bulk_sem.at[2, k], (leaf, row, before))))

    to_sibling.wait_recv()
    last[1] = hop(1, 0)

    core_copies = []

    def over_core(l, step):
        origin = lax.rem((x if l else y) + 4 - step, 4)
        group = spread.at[row, :, origin, l] if l else spread.at[row, origin, :, l]
        core_copies.append(start(remote(group, group, core_sem.at[l, step], across)))

    def relay(stage, step):
        l = stage % 2
        last[l].wait_recv()
        last[l] = hop(stage, step)
        if stage >= 2:
            over_core(l, step)

    @pl.when(col == 0)
    def _():
        loads = []
        for l in range(2):
            origin = pack if l == 0 else spread.at[row, y, x, 1]
            loads.append(pltpu.make_async_copy(
                origin.at[pl.ds(0, N)], top.at[row, l, pl.ds(0, N)], local_sem.at[1 + l]))
            loads.append(pltpu.make_async_copy(
                origin.at[pl.ds(CHUNK, 16)], top.at[row, l, pl.ds(N, 16)], local_sem.at[3 + l]))
        for load in loads:
            load.start()
        for load in loads:
            load.wait()

    def lane(n, peer):
        return pltpu.make_async_remote_copy(
            src_ref=top.at[row], dst_ref=top.at[row], send_sem=lane_sem.at[n], recv_sem=lane_sem.at[2],
            device_id=peer, device_id_type=MESH)

    lane_x, lane_y = lane(0, x_next), lane(1, y_next)

    @pl.when(jnp.logical_and(y == 0, x > 0))
    def _():
        lane_x.wait_recv()

    @pl.when(jnp.logical_and(y == 0, x < 3))
    def _():
        lane_x.start()

    @pl.when(y == 0)
    def _():
        lane_y.start()

    for step in (1, 2):
        relay(0, step)
        relay(1, step)

        @pl.when(y == step)
        def _():
            lane_y.wait_recv()
            lane_y.start()

    place.wait()
    relay(2, 0)
    relay(3, 0)

    @pl.when(y == 3)
    def _():
        lane_y.wait_recv()

    lane_core = start(remote(top.at[row], top.at[row], lane_core_sem, across))
    lane_core.wait_recv()

    def nothing():
        pass

    def both(step):
        relay(2, step)
        relay(3, step)

    hooks = ([forward, nothing, nothing, nothing], [nothing, lambda: both(1), nothing, nothing])
    factor(top, work, full, upper, linv, sinv, hooks)
    both(2)
    for l in range(2):
        last[l].wait_recv()
        over_core(l, 3)
    for copy in core_copies:
        copy.wait_recv()
    ay, ax = after // 4, lax.rem(after, 4)
    loads = [
        pltpu.make_async_copy(spread.at[:, :, :, 0, pl.ds(0, CHUNK)], own, local_sem.at[0]),
        pltpu.make_async_copy(spread.at[:, :, :, :, pl.ds(CHUNK, 16)], gains, local_sem.at[1]),
        pltpu.make_async_copy(spread.at[:, y, x, :, pl.ds(0, CHUNK)], cand.at[0], local_sem.at[2]),
        pltpu.make_async_copy(spread.at[:, ay, ax, :, pl.ds(0, CHUNK)], cand.at[1], local_sem.at[3]),
    ]
    for load in loads:
        load.start()
    for load in loads:
        load.wait()

    def candidate(n, carry):
        which, slot = n // 4, n % 4
        span = pl.ds(pl.multiple_of(slot * T, T), T)
        for l in range(2):
            rows = jnp.concatenate([cand[which, 0, l, span, :], cand[which, 1, l, span, :]], axis=1)
            value = dot(sinv[l, 0], rows, NT) + dot(sinv[l, 1], rows, NT)
            weights[n, l, 0], weights[n, l, 1] = split(value)
        return carry

    lax.fori_loop(0, 8, candidate, 0)

    first = pl.multiple_of(col * 16, 16)
    slices = jnp.concatenate([linv[0, pl.ds(first, 16), :], linv[1, pl.ds(first, 16), :]], axis=0)

    def chip(at, carry):
        cy, cx = at // 4, at % 4
        for o in range(2):
            span = pl.ds(pl.multiple_of((o * 2 + row) * T, T), T)
            rows = jnp.concatenate([own[0, cy, cx, span, :], own[1, cy, cx, span, :]], axis=1)
            pair = dot(slices, rows, NT)
            panel[o, at] = pair[:16] + pair[16:]
        for s in range(2):
            for l in range(2):
                parts = gains[s, cy, cx, l].astype(F32)
                for o in range(2):
                    gain = (parts[o : o + 1] + parts[2 + o : 3 + o]) + parts[4 + o : 5 + o]
                    reg[l, pl.ds((o * COLS + at) * 2 + s, 1), :] = gain
        return carry

    lax.fori_loop(0, COLS, chip, 0)
    panel[0, 0] = upper[pl.ds(first, 16), pl.ds(pl.multiple_of(row * T, T), T)]

    passed = []
    for k in range(PARTS):
        part = pl.ds(k * ROWS, ROWS)
        for n, (source, target) in enumerate(((kn, knx), (oth, ox), (on, onx))):
            if n != 1 or k >= FORWARDED:
                bulk[k][n].wait_recv()
            passed.append(start(remote(source.at[part], target.at[part], pass_sem.at[n, k], across)))
    for k in range(PARTS):
        bulk[k][3].wait_recv()
    for copy in passed:
        copy.wait_recv()
    for copy in sent:
        copy.wait_send()

    @pl.when(jnp.logical_and(y == 0, x < 3))
    def _():
        lane_x.wait_send()

    @pl.when(y < 3)
    def _():
        lane_y.wait_send()


def exchange(tiles, regular, cmap):
    big = jax.ShapeDtypeStruct((HALF, CHUNK, T), BF16)
    spread = jax.ShapeDtypeStruct((2, 4, 4, 2, PACK, T), BF16)
    dma = pltpu.SemaphoreType.DMA
    anywhere, vmem = pl.BlockSpec(memory_space=pltpu.HBM), pl.BlockSpec(memory_space=pltpu.VMEM)
    return pl.pallas_call(
        exchange_kernel,
        name="exchange",
        out_shape=(big,) * 7 + (
            spread,
            jax.ShapeDtypeStruct((2, COLS, 16, T), F32),
            jax.ShapeDtypeStruct((8, 2, 2, N, T), BF16),
            jax.ShapeDtypeStruct((2, 64, T), F32),
        ),
        in_specs=[anywhere, vmem, vmem],
        out_specs=(anywhere,) * 8 + (vmem,) * 3,
        scratch_shapes=[
            pltpu.VMEM((PACK, T), BF16),
            pltpu.VMEM((CHUNK, T), BF16),
            pltpu.VMEM((CHUNK, T), F32),
            pltpu.VMEM((2, 2, N + 16, T), BF16),
            pltpu.VMEM((2, 4, 4, CHUNK, T), BF16),
            pltpu.VMEM((2, 2, 2, CHUNK, T), BF16),
            pltpu.VMEM((2, 4, 4, 2, 16, T), BF16),
            pltpu.VMEM((2, T, 2 * T), F32),
            pltpu.VMEM((2, N, N), F32),
            pltpu.VMEM((N, N), F32),
            pltpu.VMEM((2, N, N), BF16),
            pltpu.VMEM((2, 2, N, N), BF16),
            dma((5,)), dma((2,)), dma((3,)), dma((2,)), dma((4, 3, 2)), dma((2, 4, 2)), dma((4, PARTS, 2)), dma((3, PARTS, 2)),
        ],
        compiler_params=pltpu.CompilerParams(collective_id=0, has_side_effects=True, vmem_limit_bytes=56 << 20),
        cost_estimate=pl.CostEstimate(flops=4 * N**3, bytes_accessed=40 << 20, transcendentals=0),
    )(tiles, regular, cmap)


def place_of(q):
    return (q // 2) % COLS, (q // (2 * COLS)) * 2 + q % 2


PAIR = 2


def parent_kernel(src, at, *refs):
    data, p_refs = refs[: 8 * PAIR], refs[8 * PAIR : 10 * PAIR]
    w_ref, reg_ref, out_ref, buf = refs[10 * PAIR :]
    row, col, half = at[0], at[1], at[3]
    diagonal = lax.broadcasted_iota(jnp.int32, (T, T), 0) == lax.broadcasted_iota(jnp.int32, (T, T), 1)
    from_rows, from_cols, spans, updates = {}, {}, {}, []
    for l in range(2):
        picks = []
        for j in range(4):
            from_col = src[l * 64 + ((j // 2) * COLS + col) * 2 + j % 2]
            chip, slot = place_of(from_col)
            far = jnp.where(chip == col, 0, 1)
            from_cols[l, j] = from_col
            spans[l, j] = pl.ds(far * CHUNK + slot, T, stride=4)
            picks.append(far * 4 + slot)
        rows = []
        for r in range(PAIR):
            from_row = src[l * 64 + 2 * (HALF * half + PAIR * pl.program_id(0) + r) + row]
            from_rows[l, r] = from_row
            mine = from_row % 2 == row
            part = data[8 * r + 4 * l : 8 * r + 4 * l + 4]

            @pl.when(mine)
            def _():
                buf[l, r, :CHUNK] = part[0][0].astype(F32)
                buf[l, r, CHUNK:] = part[1][0].astype(F32)

            @pl.when(jnp.logical_not(mine))
            def _():
                buf[l, r, :CHUNK] = part[2][0].astype(F32)
                buf[l, r, CHUNK:] = part[3][0].astype(F32)

            p_ref = p_refs[2 * r + l]
            rows.append(jnp.concatenate([p_ref[0, 0, 0], p_ref[1, 0, 0]], axis=1))
            for j in range(4):

                @pl.when(from_row == from_cols[l, j])
                def _():
                    gain = reg_ref[l, pl.ds(from_row, 1), :]
                    buf[l, r, spans[l, j], :] = buf[l, r, spans[l, j], :] + jnp.where(diagonal, gain, 0.0)

        rows = jnp.concatenate(rows, axis=0)
        high = jnp.concatenate([w_ref[pick, l, 0] for pick in picks], axis=1)
        low = jnp.concatenate([w_ref[pick, l, 1] for pick in picks], axis=1)
        updates.append(dot(rows, high, NN) + dot(rows, low, NN))
    for r in range(PAIR):
        for j in range(4):
            total = None
            for l in range(2):
                value = buf[l, r, spans[l, j], :] - updates[l][r * T : (r + 1) * T, j * T : (j + 1) * T]
                value = value.astype(BF16).astype(F32)
                value = jnp.where(jnp.logical_and(from_rows[l, r] > 0, from_cols[l, j] > 0), value, 0.0)
                total = value if total is None else total + value
            out_ref[r, pl.ds(j, T, stride=4), :] = total


def parent_out(src, at, data, gathered, weights, reg):
    def source(i, r, l, src, at):
        return src[l * 64 + 2 * (HALF * at[3] + PAIR * i + r) + at[0]]

    def chunk_spec(r, l, partner, following):
        def index(i, src, at):
            q = source(i, r, l, src, at)
            wanted = (q % 2 == at[0]) != partner
            less = 0 if l == 0 and not partner and not following else at[2]
            return (jnp.where(wanted, jnp.maximum(q // 2 - less, 0), 0), 0, 0)

        return pl.BlockSpec((1, CHUNK, T), index)

    def p_spec(r, l):
        def index(i, src, at):
            chip, slot = place_of(source(i, r, l, src, at))
            return (0, chip, l, slot, 0)

        return pl.BlockSpec((2, 1, 1, T, T), index)

    pairs = [(r, l) for r in range(PAIR) for l in range(2)]
    return pl.pallas_call(
        parent_kernel,
        name="parent_out",
        out_shape=jax.ShapeDtypeStruct((HALF, CHUNK, T), F32),
        grid_spec=pltpu.PrefetchScalarGridSpec(
            num_scalar_prefetch=2,
            grid=(HALF // PAIR,),
            in_specs=[chunk_spec(r, l, p, f) for r, l in pairs for p in (False, True) for f in (False, True)]
            + [p_spec(r, l) for r, l in pairs]
            + [
                pl.BlockSpec((8, 2, 2, N, T), lambda i, src, at: (0, 0, 0, 0, 0)),
                pl.BlockSpec((2, 64, T), lambda i, src, at: (0, 0, 0)),
            ],
            out_specs=pl.BlockSpec((PAIR, CHUNK, T), lambda i, src, at: (i, 0, 0)),
            scratch_shapes=[pltpu.VMEM((2, PAIR, 2 * CHUNK, T), F32)],
        ),
        compiler_params=pltpu.CompilerParams(vmem_limit_bytes=56 << 20),
        cost_estimate=pl.CostEstimate(flops=2 * 2 * 4096 * N * CHUNK, bytes_accessed=14 << 20, transcendentals=0),
    )(src, at, *(data * PAIR), *([gathered] * (2 * PAIR)), weights, reg)


def shards(front_tiles, regular, child_map):
    row, col = lax.axis_index("row"), lax.axis_index("col")
    half = lax.axis_index("leaf") % 2
    base = jnp.where(half == 0, 1, HALF)
    tiles = front_tiles.reshape(2 * COLS, CHUNK, T)

    cmap = jnp.pad(child_map, ((0, 0), (0, T - child_map.shape[1])), constant_values=-1)
    kn, oth, on, kx, knx, ox, onx, spread, panel, weights, reg = exchange(tiles, regular.reshape(2, T), cmap)
    gathered = spread.reshape(2, COLS, 2, PACK, T)
    data = [tiles, kn, kx, knx, oth, on, ox, onx]
    src = gathered[0, 0, :, CHUNK + 6, :64].astype(jnp.int32).reshape(-1)
    at = jnp.stack([row, col, base, half]).astype(jnp.int32)

    panel = panel.transpose(0, 1, 3, 2).reshape(1, 2, COLS, 1, T, 16)
    parent = parent_out(src, at, data, gathered, weights, reg)
    return panel, parent.reshape(1, 1, COLS, 1, T, 2, 1, 2, T)


def solution(mesh):
    return jax.shard_map(
        shards,
        mesh=mesh,
        in_specs=(
            P("leaf", None, None, "row", None, None, "col", None, None),
            P("leaf", None, "col", "row", None),
            P("leaf", None),
        ),
        out_specs=(
            P("leaf", None, None, "row", None, "col"),
            P("leaf", None, None, "row", None, None, "col", None, None),
        ),
        check_vma=False,
    )
```

```python
import jax
import jax.numpy as jnp
from jax import lax
from jax.experimental import pallas as pl
from jax.experimental.pallas import tpu as pltpu
from jax.sharding import PartitionSpec as P

T = 128
N = 256
COLS = 16
HALF = 16
CHUNK = 4 * T
BLOCK = 16
PACK = CHUNK + 16
HIGHEST = lax.Precision.HIGHEST
F32 = jnp.float32
BF16 = jnp.bfloat16


def dot(a, b, dims, precision=None):
    return lax.dot_general(a, b, (dims, ((), ())), precision=precision, preferred_element_type=F32)


NN = ((1,), (0,))
NT = ((1,), (1,))
TN = ((0,), (0,))


def unit_inverse(group, lane):
    a = {}
    for j in range(8):
        column = jnp.broadcast_to(group[:, lane + j : lane + j + 1], (8, T))
        for i in range(j, 8):
            a[i, j] = jnp.broadcast_to(column[i : i + 1, :], (8, T))
    low, inv = {}, {}
    for k in range(8):
        inv[k, k] = lax.rsqrt(a[k, k])
        for i in range(k + 1, 8):
            low[i, k] = a[i, k] * inv[k, k]
        for j in range(k + 1, 8):
            for i in range(j, 8):
                a[i, j] = a[i, j] - low[i, k] * low[j, k]
    for k in range(8):
        for i in range(k + 1, 8):
            total = low[i, k] * inv[k, k]
            for m in range(k + 1, i):
                total = total + low[i, m] * inv[m, k]
            inv[i, k] = -inv[i, i] * total
    return inv


def combined(weights, group):
    out = None
    for m in range(8):
        term = weights[m] * jnp.broadcast_to(group[m : m + 1, :], (8, T))
        out = term if out is None else out + term
    return out


def block_factor(rows, start):
    sub = lax.broadcasted_iota(jnp.int32, (8, T), 0)
    moved = pltpu.roll(rows[:, :T], lax.rem(T - start, T), axis=1)
    count = BLOCK // 8
    left = [moved[8 * g : 8 * g + 8] for g in range(count)]
    right = [rows[8 * g : 8 * g + 8, T:] for g in range(count)]
    for b in range(count):
        inv = unit_inverse(left[b], 8 * b)
        weights = []
        for m in range(8):
            weight = jnp.zeros((8, T), F32)
            for k in range(m, 8):
                weight = jnp.where(sub == k, inv[k, m], weight)
            weights.append(weight)
        left_next, right_next = combined(weights, left[b]), combined(weights, right[b])
        for g in range(b + 1, count):
            columns = [jnp.broadcast_to(left[g][:, 8 * b + k : 8 * b + k + 1], (8, T)) for k in range(8)]
            lows = []
            for m in range(8):
                low = columns[0] * inv[m, 0]
                for k in range(1, m + 1):
                    low = low + columns[k] * inv[m, k]
                lows.append(low)
            left[g] = left[g] - combined(lows, left_next)
            right[g] = right[g] - combined(lows, right_next)
        left[b], right[b] = left_next, right_next
    upper = pltpu.roll(jnp.concatenate(left, axis=0), start, axis=1)
    lane = lax.broadcasted_iota(jnp.int32, (BLOCK, T), 1)
    upper = jnp.where(lane >= start + lax.broadcasted_iota(jnp.int32, (BLOCK, T), 0), upper, 0.0)
    later = jnp.where(lane >= start + BLOCK, upper, 0.0)
    return jnp.concatenate([upper, jnp.concatenate(right, axis=0)], axis=1), later


def split(value):
    high = value.astype(BF16)
    return high, (value - high.astype(F32)).astype(BF16)


def eliminate(work, hooks):
    def body(b, carry):
        start = pl.multiple_of(b * BLOCK, BLOCK)
        done = [block_factor(work[l, pl.ds(start, BLOCK), :], start) for l in range(2)]
        for l in range(2):
            rows, later = done[l]
            high, low = split(rows)
            later_high, later_low = split(later)
            left = jnp.concatenate([later_high, later_high, later_low], axis=0)
            right = jnp.concatenate([high, low, high], axis=0)
            work[l] = work[l] - dot(left, right, TN)
            work[l, pl.ds(start, BLOCK), :] = rows
        return carry

    count, steps = len(hooks), T // BLOCK
    for n, hook in enumerate(hooks):
        lax.fori_loop(n * steps // count, (n + 1) * steps // count, body, 0)
        hook()


def factor(top, work, full, upper, linv, sinv, hooks):
    eye = lax.broadcasted_iota(jnp.int32, (T, T), 0) == lax.broadcasted_iota(jnp.int32, (T, T), 1)
    one = jnp.where(eye, 1.0, 0.0).astype(F32)

    def block(q, s, l):
        value = top[s, l, q * T : (q + 1) * T, :].astype(F32)
        if q == s:
            parts = top[s, l, N : N + 16, :].astype(F32)
            gain = (parts[0:1] + parts[2:3]) + parts[4:5]
            value = value + jnp.where(eye, gain, 0.0)
        return value

    for l in range(2):
        work[l, :, :T] = block(0, 0, l)
        work[l, :, T:] = one
    eliminate(work, hooks[0])
    for l in range(2):
        inverse = work[l, :, T:]
        across = dot(inverse, block(0, 1, l), NN, HIGHEST)
        if l == 0:
            upper[:, :T] = jnp.concatenate([work[l, :, :T], jnp.zeros((T, T), F32)], axis=0)
            upper[:T, T:] = across
        full[l, :T, :T] = inverse
        full[l, :T, T:] = jnp.zeros((T, T), F32)
        full[l, T:, :T] = dot(across, inverse, TN, HIGHEST)
        work[l, :, :T] = block(1, 1, l) - dot(across, across, TN, HIGHEST)
        work[l, :, T:] = one
    eliminate(work, hooks[1])
    for l in range(2):
        inverse = work[l, :, T:]
        if l == 0:
            upper[T:, T:] = work[l, :, :T]
        full[l, T:, :T] = -dot(inverse, full[l, T:, :T], NN, HIGHEST)
        full[l, T:, T:] = inverse
        whole = full[l]
        sinv[l, 0], sinv[l, 1] = split(dot(whole, whole, TN, HIGHEST))
    linv[0], linv[1] = split(full[0])


PARTS = 4
FORWARDED = 1
ROWS = HALF // PARTS
MESH = pl.DeviceIdType.MESH


def exchange_kernel(
    tiles, regular, cmap, kn, oth, on, kx, knx, ox, onx, spread, panel, weights, reg,
    pack, raw, wide, top, own, cand, gains, work, full, upper, linv, sinv,
    local_sem, z_sem, lane_sem, lane_core_sem, ring_sem, core_sem, bulk_sem, pass_sem,
):
    leaf, row, col = lax.axis_index("leaf"), lax.axis_index("row"), lax.axis_index("col")
    y, x = col // 4, col % 4
    sibling = leaf + 1 - 2 * (leaf % 2)
    before, after = lax.rem(col + COLS - 1, COLS), lax.rem(col + 1, COLS)
    half = leaf % 2
    keep = 1 + half * (HALF - 1)
    send = HALF - half * (HALF - 1)
    across = (leaf, 1 - row, col)
    x_next = (leaf, row, y * 4 + lax.rem(x + 1, 4))
    y_next = (leaf, row, lax.rem(y + 1, 4) * 4 + x)

    peers = [(sibling, row, col), (sibling, row, before), (sibling, row, after)]
    peers += [(leaf, row, before), (leaf, row, after), across]
    peers += [(leaf, row, y * 4 + lax.rem(x + d, 4)) for d in (1, 3)]
    peers += [(leaf, row, lax.rem(y + d, 4) * 4 + x) for d in (1, 3)]
    first_rows = pltpu.make_async_copy(tiles.at[0], raw, local_sem.at[0])
    first_rows.start()
    barrier = pltpu.get_barrier_semaphore()
    for peer in peers:
        pl.semaphore_signal(barrier, inc=1, device_id=peer, device_id_type=MESH)
    pl.semaphore_wait(barrier, len(peers))

    def remote(source, target, sems, peer):
        return pltpu.make_async_remote_copy(
            src_ref=source, dst_ref=target, send_sem=sems.at[0], recv_sem=sems.at[1],
            device_id=peer, device_id_type=MESH,
        )

    sent = []

    def start(copy):
        copy.start()
        sent.append(copy)
        return copy

    def hop(stage, step):
        l = stage % 2
        along_x = (stage // 2) == l
        origin = lax.rem((x if along_x else y) + 4 - step, 4)
        if stage < 2:
            place = spread.at[row, y, origin, l] if along_x else spread.at[row, origin, x, l]
        else:
            place = spread.at[row, :, origin, l] if along_x else spread.at[row, origin, :, l]
        source = pack if stage == 0 and step == 0 else place
        return start(remote(source, place, ring_sem.at[stage, step], x_next if along_x else y_next))

    bulk = []
    for k in range(PARTS):
        kept, part = tiles.at[pl.ds(keep + k * ROWS, ROWS)], pl.ds(k * ROWS, ROWS)
        bulk.append([
            start(remote(kept, kn.at[part], bulk_sem.at[0, k], (leaf, row, before))),
            start(remote(kept, kx.at[part], bulk_sem.at[3, k], across)),
        ])

    first_rows.wait()
    wide[...] = raw[...].astype(F32)
    for j in range(4):
        pack[j * T : (j + 1) * T, :] = wide[pl.ds(j, T, stride=4), :].T.astype(BF16)
    value = regular[...]
    high = value.astype(BF16).astype(F32)
    rest = value - high
    middle = rest.astype(BF16).astype(F32)
    lane = lax.broadcasted_iota(jnp.int32, (T, T), 1)
    match = cmap[...] == lax.broadcasted_iota(jnp.int32, (T, T), 0)
    source = jnp.where(match, lane + 2, 0).astype(F32).T
    source = jnp.sum(source, axis=0, keepdims=True)
    pack[CHUNK:, :] = jnp.concatenate([high, middle, rest - middle, source, jnp.zeros((9, T), F32)], axis=0).astype(BF16)

    to_sibling = start(remote(pack, spread.at[row, y, x, 1], z_sem, (sibling, row, col)))
    last = [hop(0, 0), None]
    place = pltpu.make_async_copy(pack, spread.at[row, y, x, 0], local_sem.at[0])
    place.start()
    for k in range(PARTS):
        gone, part = tiles.at[pl.ds(send + k * ROWS, ROWS)], pl.ds(k * ROWS, ROWS)
        bulk[k].insert(1, start(remote(gone, oth.at[part], bulk_sem.at[1, k], (sibling, row, col))))
        if k >= FORWARDED:
            bulk[k].insert(2, start(remote(gone, on.at[part], bulk_sem.at[2, k], (sibling, row, before))))

    def forward():
        for k in range(FORWARDED):
            part = pl.ds(k * ROWS, ROWS)
            bulk[k][1].wait_recv()
            bulk[k].insert(2, start(remote(oth.at[part], on.at[part], bulk_sem.at[2, k], (leaf, row, before))))

    to_sibling.wait_recv()
    last[1] = hop(1, 0)

    core_copies = []

    def over_core(l, step):
        origin = lax.rem((x if l else y) + 4 - step, 4)
        group = spread.at[row, :, origin, l] if l else spread.at[row, origin, :, l]
        core_copies.append(start(remote(group, group, core_sem.at[l, step], across)))

    def relay(stage, step):
        l = stage % 2
        last[l].wait_recv()
        last[l] = hop(stage, step)
        if stage >= 2:
            over_core(l, step)

    @pl.when(col == 0)
    def _():
        loads = []
        for l in range(2):
            origin = pack if l == 0 else spread.at[row, y, x, 1]
            loads.append(pltpu.make_async_copy(
                origin.at[pl.ds(0, N)], top.at[row, l, pl.ds(0, N)], local_sem.at[1 + l]))
            loads.append(pltpu.make_async_copy(
                origin.at[pl.ds(CHUNK, 16)], top.at[row, l, pl.ds(N, 16)], local_sem.at[3 + l]))
        for load in loads:
            load.start()
        for load in loads:
            load.wait()

    def lane(n, peer):
        return pltpu.make_async_remote_copy(
            src_ref=top.at[row], dst_ref=top.at[row], send_sem=lane_sem.at[n], recv_sem=lane_sem.at[2],
            device_id=peer, device_id_type=MESH)

    lane_x, lane_y = lane(0, x_next), lane(1, y_next)

    @pl.when(jnp.logical_and(y == 0, x > 0))
    def _():
        lane_x.wait_recv()

    @pl.when(jnp.logical_and(y == 0, x < 3))
    def _():
        lane_x.start()

    @pl.when(y == 0)
    def _():
        lane_y.start()

    for step in (1, 2):
        relay(0, step)
        relay(1, step)

        @pl.when(y == step)
        def _():
            lane_y.wait_recv()
            lane_y.start()

    place.wait()
    relay(2, 0)
    relay(3, 0)

    @pl.when(y == 3)
    def _():
        lane_y.wait_recv()

    lane_core = start(remote(top.at[row], top.at[row], lane_core_sem, across))
    lane_core.wait_recv()

    def nothing():
        pass

    def both(step):
        relay(2, step)
        relay(3, step)

    hooks = ([forward, nothing, nothing, nothing], [nothing, lambda: both(1), nothing, nothing])
    factor(top, work, full, upper, linv, sinv, hooks)
    both(2)
    first = pl.multiple_of(col * 16, 16)
    slices = jnp.concatenate([linv[0, pl.ds(first, 16), :], linv[1, pl.ds(first, 16), :]], axis=0)

    def panel_groups(steps):
        loads = []
        for n, step in enumerate(steps):
            cy = lax.rem(y + 4 - step, 4)
            load = pltpu.make_async_copy(spread.at[:, cy, :, 0, pl.ds(0, CHUNK)], own.at[:, cy], local_sem.at[n])
            load.start()
            loads.append(load)
        for load in loads:
            load.wait()

        def chip(n, carry):
            cy, cx = lax.rem(y + 4 - (steps[0] + n // 4), 4), n % 4
            for o in range(2):
                span = pl.ds(pl.multiple_of((o * 2 + row) * T, T), T)
                rows = jnp.concatenate([own[0, cy, cx, span, :], own[1, cy, cx, span, :]], axis=1)
                pair = dot(slices, rows, NT)
                panel[o, cy * 4 + cx] = pair[:16] + pair[16:]
            return carry

        lax.fori_loop(0, 4 * len(steps), chip, 0)

    for copy in core_copies:
        copy.wait_recv()
    panel_groups((0, 1, 2))
    for l in range(2):
        last[l].wait_recv()
        over_core(l, 3)
    for copy in core_copies[6:]:
        copy.wait_recv()
    panel_groups((3,))
    ay, ax = after // 4, lax.rem(after, 4)
    loads = [
        pltpu.make_async_copy(spread.at[:, :, :, :, pl.ds(CHUNK, 16)], gains, local_sem.at[1]),
        pltpu.make_async_copy(spread.at[:, y, x, :, pl.ds(0, CHUNK)], cand.at[0], local_sem.at[2]),
        pltpu.make_async_copy(spread.at[:, ay, ax, :, pl.ds(0, CHUNK)], cand.at[1], local_sem.at[3]),
    ]
    for load in loads:
        load.start()
    for load in loads:
        load.wait()

    def candidate(n, carry):
        which, slot = n // 4, n % 4
        span = pl.ds(pl.multiple_of(slot * T, T), T)
        for l in range(2):
            rows = jnp.concatenate([cand[which, 0, l, span, :], cand[which, 1, l, span, :]], axis=1)
            value = dot(sinv[l, 0], rows, NT) + dot(sinv[l, 1], rows, NT)
            weights[n, l, 0], weights[n, l, 1] = split(value)
        return carry

    lax.fori_loop(0, 8, candidate, 0)

    def chip_gains(at, carry):
        cy, cx = at // 4, at % 4
        for s in range(2):
            for l in range(2):
                parts = gains[s, cy, cx, l].astype(F32)
                for o in range(2):
                    gain = (parts[o : o + 1] + parts[2 + o : 3 + o]) + parts[4 + o : 5 + o]
                    reg[l, pl.ds((o * COLS + at) * 2 + s, 1), :] = gain
        return carry

    lax.fori_loop(0, COLS, chip_gains, 0)
    panel[0, 0] = upper[pl.ds(first, 16), pl.ds(pl.multiple_of(row * T, T), T)]

    passed = []
    for k in range(PARTS):
        part = pl.ds(k * ROWS, ROWS)
        for n, (source, target) in enumerate(((kn, knx), (oth, ox), (on, onx))):
            if n != 1 or k >= FORWARDED:
                bulk[k][n].wait_recv()
            passed.append(start(remote(source.at[part], target.at[part], pass_sem.at[n, k], across)))
    for k in range(PARTS):
        bulk[k][3].wait_recv()
    for copy in passed:
        copy.wait_recv()
    for copy in sent:
        copy.wait_send()

    @pl.when(jnp.logical_and(y == 0, x < 3))
    def _():
        lane_x.wait_send()

    @pl.when(y < 3)
    def _():
        lane_y.wait_send()


def exchange(tiles, regular, cmap):
    big = jax.ShapeDtypeStruct((HALF, CHUNK, T), BF16)
    spread = jax.ShapeDtypeStruct((2, 4, 4, 2, PACK, T), BF16)
    dma = pltpu.SemaphoreType.DMA
    anywhere, vmem = pl.BlockSpec(memory_space=pltpu.HBM), pl.BlockSpec(memory_space=pltpu.VMEM)
    return pl.pallas_call(
        exchange_kernel,
        name="exchange",
        out_shape=(big,) * 7 + (
            spread,
            jax.ShapeDtypeStruct((2, COLS, 16, T), F32),
            jax.ShapeDtypeStruct((8, 2, 2, N, T), BF16),
            jax.ShapeDtypeStruct((2, 64, T), F32),
        ),
        in_specs=[anywhere, vmem, vmem],
        out_specs=(anywhere,) * 8 + (vmem,) * 3,
        scratch_shapes=[
            pltpu.VMEM((PACK, T), BF16),
            pltpu.VMEM((CHUNK, T), BF16),
            pltpu.VMEM((CHUNK, T), F32),
            pltpu.VMEM((2, 2, N + 16, T), BF16),
            pltpu.VMEM((2, 4, 4, CHUNK, T), BF16),
            pltpu.VMEM((2, 2, 2, CHUNK, T), BF16),
            pltpu.VMEM((2, 4, 4, 2, 16, T), BF16),
            pltpu.VMEM((2, T, 2 * T), F32),
            pltpu.VMEM((2, N, N), F32),
            pltpu.VMEM((N, N), F32),
            pltpu.VMEM((2, N, N), BF16),
            pltpu.VMEM((2, 2, N, N), BF16),
            dma((5,)), dma((2,)), dma((3,)), dma((2,)), dma((4, 3, 2)), dma((2, 4, 2)), dma((4, PARTS, 2)), dma((3, PARTS, 2)),
        ],
        compiler_params=pltpu.CompilerParams(collective_id=0, has_side_effects=True, vmem_limit_bytes=56 << 20),
        cost_estimate=pl.CostEstimate(flops=4 * N**3, bytes_accessed=40 << 20, transcendentals=0),
    )(tiles, regular, cmap)


def place_of(q):
    return (q >> 1) & (COLS - 1), ((q >> 5) << 1) + (q & 1)


PAIR = 4


def parent_kernel(src, at, *refs):
    data, p_refs = refs[: 8 * PAIR], refs[8 * PAIR : 10 * PAIR]
    w_ref, reg_ref, out_ref, buf = refs[10 * PAIR :]
    row, col, half = at[0], at[1], at[3]
    diagonal = lax.broadcasted_iota(jnp.int32, (T, T), 0) == lax.broadcasted_iota(jnp.int32, (T, T), 1)
    from_rows, from_cols, spans, updates = {}, {}, {}, []
    for l in range(2):
        picks = []
        for j in range(4):
            from_col = src[l * 64 + ((j // 2) * COLS + col) * 2 + j % 2]
            chip, slot = place_of(from_col)
            far = jnp.where(chip == col, 0, 1)
            from_cols[l, j] = from_col
            spans[l, j] = pl.ds(far * CHUNK + slot, T, stride=4)
            picks.append(far * 4 + slot)
        rows = []
        for r in range(PAIR):
            from_row = src[l * 64 + 2 * (HALF * half + PAIR * pl.program_id(0) + r) + row]
            from_rows[l, r] = from_row
            mine = (from_row & 1) == row
            part = data[8 * r + 4 * l : 8 * r + 4 * l + 4]

            @pl.when(mine)
            def _():
                buf[l, r, :CHUNK] = part[0][0].astype(F32)
                buf[l, r, CHUNK:] = part[1][0].astype(F32)

            @pl.when(jnp.logical_not(mine))
            def _():
                buf[l, r, :CHUNK] = part[2][0].astype(F32)
                buf[l, r, CHUNK:] = part[3][0].astype(F32)

            p_ref = p_refs[2 * r + l]
            rows.append(jnp.concatenate([p_ref[0, 0, 0], p_ref[1, 0, 0]], axis=1))
            for j in range(4):

                @pl.when(from_row == from_cols[l, j])
                def _():
                    gain = reg_ref[l, pl.ds(from_row, 1), :]
                    buf[l, r, spans[l, j], :] = buf[l, r, spans[l, j], :] + jnp.where(diagonal, gain, 0.0)

        rows = jnp.concatenate(rows, axis=0)
        high = jnp.concatenate([w_ref[pick, l, 0] for pick in picks], axis=1)
        low = jnp.concatenate([w_ref[pick, l, 1] for pick in picks], axis=1)
        updates.append(dot(rows, high, NN) + dot(rows, low, NN))
    for r in range(PAIR):
        for j in range(4):
            total = None
            for l in range(2):
                value = buf[l, r, spans[l, j], :] - updates[l][r * T : (r + 1) * T, j * T : (j + 1) * T]
                value = value.astype(BF16).astype(F32)
                value = jnp.where(jnp.logical_and(from_rows[l, r] > 0, from_cols[l, j] > 0), value, 0.0)
                total = value if total is None else total + value
            out_ref[r, pl.ds(j, T, stride=4), :] = total


def parent_out(src, at, data, gathered, weights, reg):
    def source(i, r, l, src, at):
        return src[l * 64 + 2 * (HALF * at[3] + PAIR * i + r) + at[0]]

    def chunk_spec(r, l, partner, following):
        def index(i, src, at):
            q = source(i, r, l, src, at)
            wanted = (q & 1) == (at[0] ^ int(partner))
            less = 0 if l == 0 and not partner and not following else at[2]
            return (jnp.where(wanted, jnp.maximum((q >> 1) - less, 0), 0), 0, 0)

        return pl.BlockSpec((1, CHUNK, T), index)

    def p_spec(r, l):
        def index(i, src, at):
            chip, slot = place_of(source(i, r, l, src, at))
            return (0, chip, l, slot, 0)

        return pl.BlockSpec((2, 1, 1, T, T), index)

    pairs = [(r, l) for r in range(PAIR) for l in range(2)]
    return pl.pallas_call(
        parent_kernel,
        name="parent_out",
        out_shape=jax.ShapeDtypeStruct((HALF, CHUNK, T), F32),
        grid_spec=pltpu.PrefetchScalarGridSpec(
            num_scalar_prefetch=2,
            grid=(HALF // PAIR,),
            in_specs=[chunk_spec(r, l, p, f) for r, l in pairs for p in (False, True) for f in (False, True)]
            + [p_spec(r, l) for r, l in pairs]
            + [
                pl.BlockSpec((8, 2, 2, N, T), lambda i, src, at: (0, 0, 0, 0, 0)),
                pl.BlockSpec((2, 64, T), lambda i, src, at: (0, 0, 0)),
            ],
            out_specs=pl.BlockSpec((PAIR, CHUNK, T), lambda i, src, at: (i, 0, 0)),
            scratch_shapes=[pltpu.VMEM((2, PAIR, 2 * CHUNK, T), F32)],
        ),
        compiler_params=pltpu.CompilerParams(vmem_limit_bytes=56 << 20),
        cost_estimate=pl.CostEstimate(flops=2 * 2 * 4096 * N * CHUNK, bytes_accessed=14 << 20, transcendentals=0),
    )(src, at, *(data * PAIR), *([gathered] * (2 * PAIR)), weights, reg)


def shards(front_tiles, regular, child_map):
    row, col = lax.axis_index("row"), lax.axis_index("col")
    half = lax.axis_index("leaf") % 2
    base = jnp.where(half == 0, 1, HALF)
    tiles = front_tiles.reshape(2 * COLS, CHUNK, T)

    cmap = jnp.pad(child_map, ((0, 0), (0, T - child_map.shape[1])), constant_values=-1)
    kn, oth, on, kx, knx, ox, onx, spread, panel, weights, reg = exchange(tiles, regular.reshape(2, T), cmap)
    gathered = spread.reshape(2, COLS, 2, PACK, T)
    data = [tiles, kn, kx, knx, oth, on, ox, onx]
    src = gathered[0, 0, :, CHUNK + 6, :64].astype(jnp.int32).reshape(-1)
    at = jnp.stack([row, col, base, half]).astype(jnp.int32)

    panel = panel.transpose(0, 1, 3, 2).reshape(1, 2, COLS, 1, T, 16)
    parent = parent_out(src, at, data, gathered, weights, reg)
    return panel, parent.reshape(1, 1, COLS, 1, T, 2, 1, 2, T)


def solution(mesh):
    return jax.shard_map(
        shards,
        mesh=mesh,
        in_specs=(
            P("leaf", None, None, "row", None, None, "col", None, None),
            P("leaf", None, "col", "row", None),
            P("leaf", None),
        ),
        out_specs=(
            P("leaf", None, None, "row", None, "col"),
            P("leaf", None, None, "row", None, None, "col", None, None),
        ),
        check_vma=False,
    )
```

```python
import jax
import jax.numpy as jnp
from jax import lax
from jax.experimental import pallas as pl
from jax.experimental.pallas import tpu as pltpu
from jax.sharding import PartitionSpec as P

T = 128
N = 256
COLS = 16
HALF = 16
CHUNK = 4 * T
BLOCK = 16
PACK = CHUNK + 16
HIGHEST = lax.Precision.HIGHEST
F32 = jnp.float32
BF16 = jnp.bfloat16


def dot(a, b, dims, precision=None):
    return lax.dot_general(a, b, (dims, ((), ())), precision=precision, preferred_element_type=F32)


NN = ((1,), (0,))
NT = ((1,), (1,))
TN = ((0,), (0,))


def unit_inverse(group, lane):
    a = {}
    for j in range(8):
        column = jnp.broadcast_to(group[:, lane + j : lane + j + 1], (8, T))
        for i in range(j, 8):
            a[i, j] = jnp.broadcast_to(column[i : i + 1, :], (8, T))
    low, inv = {}, {}
    for k in range(8):
        inv[k, k] = lax.rsqrt(a[k, k])
        for i in range(k + 1, 8):
            low[i, k] = a[i, k] * inv[k, k]
        for j in range(k + 1, 8):
            for i in range(j, 8):
                a[i, j] = a[i, j] - low[i, k] * low[j, k]
    for k in range(8):
        for i in range(k + 1, 8):
            total = low[i, k] * inv[k, k]
            for m in range(k + 1, i):
                total = total + low[i, m] * inv[m, k]
            inv[i, k] = -inv[i, i] * total
    return inv


def combined(weights, group):
    out = None
    for m in range(8):
        term = weights[m] * jnp.broadcast_to(group[m : m + 1, :], (8, T))
        out = term if out is None else out + term
    return out


def block_factor(rows, start):
    sub = lax.broadcasted_iota(jnp.int32, (8, T), 0)
    moved = pltpu.roll(rows[:, :T], lax.rem(T - start, T), axis=1)
    count = BLOCK // 8
    left = [moved[8 * g : 8 * g + 8] for g in range(count)]
    right = [rows[8 * g : 8 * g + 8, T:] for g in range(count)]
    for b in range(count):
        inv = unit_inverse(left[b], 8 * b)
        weights = []
        for m in range(8):
            weight = jnp.zeros((8, T), F32)
            for k in range(m, 8):
                weight = jnp.where(sub == k, inv[k, m], weight)
            weights.append(weight)
        left_next, right_next = combined(weights, left[b]), combined(weights, right[b])
        for g in range(b + 1, count):
            columns = [jnp.broadcast_to(left[g][:, 8 * b + k : 8 * b + k + 1], (8, T)) for k in range(8)]
            lows = []
            for m in range(8):
                low = columns[0] * inv[m, 0]
                for k in range(1, m + 1):
                    low = low + columns[k] * inv[m, k]
                lows.append(low)
            left[g] = left[g] - combined(lows, left_next)
            right[g] = right[g] - combined(lows, right_next)
        left[b], right[b] = left_next, right_next
    upper = pltpu.roll(jnp.concatenate(left, axis=0), start, axis=1)
    lane = lax.broadcasted_iota(jnp.int32, (BLOCK, T), 1)
    upper = jnp.where(lane >= start + lax.broadcasted_iota(jnp.int32, (BLOCK, T), 0), upper, 0.0)
    later = jnp.where(lane >= start + BLOCK, upper, 0.0)
    return jnp.concatenate([upper, jnp.concatenate(right, axis=0)], axis=1), later


def split(value):
    high = value.astype(BF16)
    return high, (value - high.astype(F32)).astype(BF16)


def eliminate(work, hooks):
    def body(b, carry):
        start = pl.multiple_of(b * BLOCK, BLOCK)
        done = [block_factor(work[l, pl.ds(start, BLOCK), :], start) for l in range(2)]
        for l in range(2):
            rows, later = done[l]
            high, low = split(rows)
            later_high, later_low = split(later)
            left = jnp.concatenate([later_high, later_high, later_low], axis=0)
            right = jnp.concatenate([high, low, high], axis=0)
            work[l] = work[l] - dot(left, right, TN)
            work[l, pl.ds(start, BLOCK), :] = rows
        return carry

    count, steps = len(hooks), T // BLOCK
    for n, hook in enumerate(hooks):
        lax.fori_loop(n * steps // count, (n + 1) * steps // count, body, 0)
        hook()


def factor(top, work, full, upper, linv, sinv, hooks):
    eye = lax.broadcasted_iota(jnp.int32, (T, T), 0) == lax.broadcasted_iota(jnp.int32, (T, T), 1)
    one = jnp.where(eye, 1.0, 0.0).astype(F32)

    def block(q, s, l):
        value = top[s, l, q * T : (q + 1) * T, :].astype(F32)
        if q == s:
            parts = top[s, l, N : N + 16, :].astype(F32)
            gain = (parts[0:1] + parts[2:3]) + parts[4:5]
            value = value + jnp.where(eye, gain, 0.0)
        return value

    for l in range(2):
        work[l, :, :T] = block(0, 0, l)
        work[l, :, T:] = one
    eliminate(work, hooks[0])
    for l in range(2):
        inverse = work[l, :, T:]
        across = dot(inverse, block(0, 1, l), NN, HIGHEST)
        if l == 0:
            upper[:, :T] = jnp.concatenate([work[l, :, :T], jnp.zeros((T, T), F32)], axis=0)
            upper[:T, T:] = across
        full[l, :T, :T] = inverse
        full[l, :T, T:] = jnp.zeros((T, T), F32)
        full[l, T:, :T] = dot(across, inverse, TN, HIGHEST)
        work[l, :, :T] = block(1, 1, l) - dot(across, across, TN, HIGHEST)
        work[l, :, T:] = one
    eliminate(work, hooks[1])
    for l in range(2):
        inverse = work[l, :, T:]
        if l == 0:
            upper[T:, T:] = work[l, :, :T]
        full[l, T:, :T] = -dot(inverse, full[l, T:, :T], NN, HIGHEST)
        full[l, T:, T:] = inverse
        whole = full[l]
        sinv[l, 0], sinv[l, 1] = split(dot(whole, whole, TN, HIGHEST))
    linv[0], linv[1] = split(full[0])


PARTS = 4
FORWARDED = 3
ROWS = HALF // PARTS
MESH = pl.DeviceIdType.MESH


def exchange_kernel(
    tiles, regular, cmap, kn, oth, on, kx, knx, ox, onx, spread, panel, weights, reg,
    pack, raw, wide, top, own, cand, gains, work, full, upper, linv, sinv,
    local_sem, z_sem, lane_sem, lane_core_sem, ring_sem, core_sem, bulk_sem, pass_sem,
):
    leaf, row, col = lax.axis_index("leaf"), lax.axis_index("row"), lax.axis_index("col")
    y, x = col // 4, col % 4
    sibling = leaf + 1 - 2 * (leaf % 2)
    before, after = lax.rem(col + COLS - 1, COLS), lax.rem(col + 1, COLS)
    half = leaf % 2
    keep = 1 + half * (HALF - 1)
    send = HALF - half * (HALF - 1)
    across = (leaf, 1 - row, col)
    x_next = (leaf, row, y * 4 + lax.rem(x + 1, 4))
    y_next = (leaf, row, lax.rem(y + 1, 4) * 4 + x)

    peers = [(sibling, row, col), (sibling, row, before), (sibling, row, after)]
    peers += [(leaf, row, before), (leaf, row, after), across]
    peers += [(leaf, row, y * 4 + lax.rem(x + d, 4)) for d in (1, 3)]
    peers += [(leaf, row, lax.rem(y + d, 4) * 4 + x) for d in (1, 3)]
    first_rows = pltpu.make_async_copy(tiles.at[0], raw, local_sem.at[0])
    first_rows.start()
    barrier = pltpu.get_barrier_semaphore()
    for peer in peers:
        pl.semaphore_signal(barrier, inc=1, device_id=peer, device_id_type=MESH)
    pl.semaphore_wait(barrier, len(peers))

    def remote(source, target, sems, peer):
        return pltpu.make_async_remote_copy(
            src_ref=source, dst_ref=target, send_sem=sems.at[0], recv_sem=sems.at[1],
            device_id=peer, device_id_type=MESH,
        )

    sent = []

    def start(copy):
        copy.start()
        sent.append(copy)
        return copy

    def hop(stage, step):
        l = stage % 2
        along_x = (stage // 2) == l
        origin = lax.rem((x if along_x else y) + 4 - step, 4)
        if stage < 2:
            place = spread.at[row, y, origin, l] if along_x else spread.at[row, origin, x, l]
        else:
            place = spread.at[row, :, origin, l] if along_x else spread.at[row, origin, :, l]
        source = pack if stage == 0 and step == 0 else place
        return start(remote(source, place, ring_sem.at[stage, step], x_next if along_x else y_next))

    bulk = []
    for k in range(PARTS):
        kept, part = tiles.at[pl.ds(keep + k * ROWS, ROWS)], pl.ds(k * ROWS, ROWS)
        bulk.append([
            start(remote(kept, kn.at[part], bulk_sem.at[0, k], (leaf, row, before))),
            start(remote(kept, kx.at[part], bulk_sem.at[3, k], across)),
        ])

    first_rows.wait()
    wide[...] = raw[...].astype(F32)
    for j in range(4):
        pack[j * T : (j + 1) * T, :] = wide[pl.ds(j, T, stride=4), :].T.astype(BF16)
    value = regular[...]
    high = value.astype(BF16).astype(F32)
    rest = value - high
    middle = rest.astype(BF16).astype(F32)
    lane = lax.broadcasted_iota(jnp.int32, (T, T), 1)
    match = cmap[...] == lax.broadcasted_iota(jnp.int32, (T, T), 0)
    source = jnp.where(match, lane + 2, 0).astype(F32).T
    source = jnp.sum(source, axis=0, keepdims=True)
    pack[CHUNK:, :] = jnp.concatenate([high, middle, rest - middle, source, jnp.zeros((9, T), F32)], axis=0).astype(BF16)

    to_sibling = start(remote(pack, spread.at[row, y, x, 1], z_sem, (sibling, row, col)))
    last = [hop(0, 0), None]
    place = pltpu.make_async_copy(pack, spread.at[row, y, x, 0], local_sem.at[0])
    place.start()
    for k in range(PARTS):
        gone, part = tiles.at[pl.ds(send + k * ROWS, ROWS)], pl.ds(k * ROWS, ROWS)
        bulk[k].insert(1, start(remote(gone, oth.at[part], bulk_sem.at[1, k], (sibling, row, col))))
        if k >= FORWARDED:
            bulk[k].insert(2, start(remote(gone, on.at[part], bulk_sem.at[2, k], (sibling, row, before))))

    def forward():
        for k in range(FORWARDED):
            part = pl.ds(k * ROWS, ROWS)
            bulk[k][1].wait_recv()
            bulk[k].insert(2, start(remote(oth.at[part], on.at[part], bulk_sem.at[2, k], (leaf, row, before))))

    to_sibling.wait_recv()
    last[1] = hop(1, 0)

    core_copies = []

    def over_core(l, step):
        origin = lax.rem((x if l else y) + 4 - step, 4)
        group = spread.at[row, :, origin, l] if l else spread.at[row, origin, :, l]
        core_copies.append(start(remote(group, group, core_sem.at[l, step], across)))

    def relay(stage, step):
        l = stage % 2
        last[l].wait_recv()
        last[l] = hop(stage, step)
        if stage >= 2:
            over_core(l, step)

    @pl.when(col == 0)
    def _():
        loads = []
        for l in range(2):
            origin = pack if l == 0 else spread.at[row, y, x, 1]
            loads.append(pltpu.make_async_copy(
                origin.at[pl.ds(0, N)], top.at[row, l, pl.ds(0, N)], local_sem.at[1 + l]))
            loads.append(pltpu.make_async_copy(
                origin.at[pl.ds(CHUNK, 16)], top.at[row, l, pl.ds(N, 16)], local_sem.at[3 + l]))
        for load in loads:
            load.start()
        for load in loads:
            load.wait()

    def lane(n, peer):
        return pltpu.make_async_remote_copy(
            src_ref=top.at[row], dst_ref=top.at[row], send_sem=lane_sem.at[n], recv_sem=lane_sem.at[2],
            device_id=peer, device_id_type=MESH)

    lane_x, lane_y = lane(0, x_next), lane(1, y_next)

    @pl.when(jnp.logical_and(y == 0, x > 0))
    def _():
        lane_x.wait_recv()

    @pl.when(jnp.logical_and(y == 0, x < 3))
    def _():
        lane_x.start()

    @pl.when(y == 0)
    def _():
        lane_y.start()

    for step in (1, 2):
        relay(0, step)
        relay(1, step)

        @pl.when(y == step)
        def _():
            lane_y.wait_recv()
            lane_y.start()

    place.wait()
    relay(2, 0)
    relay(3, 0)

    @pl.when(y == 3)
    def _():
        lane_y.wait_recv()

    lane_core = start(remote(top.at[row], top.at[row], lane_core_sem, across))
    lane_core.wait_recv()

    def nothing():
        pass

    def both(step):
        relay(2, step)
        relay(3, step)

    hooks = ([forward, nothing, nothing, nothing], [nothing, lambda: both(1), nothing, nothing])
    factor(top, work, full, upper, linv, sinv, hooks)
    both(2)
    first = pl.multiple_of(col * 16, 16)
    slices = jnp.concatenate([linv[0, pl.ds(first, 16), :], linv[1, pl.ds(first, 16), :]], axis=0)

    def panel_groups(steps):
        loads = []
        for n, step in enumerate(steps):
            cy = lax.rem(y + 4 - step, 4)
            load = pltpu.make_async_copy(spread.at[:, cy, :, 0, pl.ds(0, CHUNK)], own.at[:, cy], local_sem.at[n])
            load.start()
            loads.append(load)
        for load in loads:
            load.wait()

        def chip(n, carry):
            cy, cx = lax.rem(y + 4 - (steps[0] + n // 4), 4), n % 4
            for o in range(2):
                span = pl.ds(pl.multiple_of((o * 2 + row) * T, T), T)
                rows = jnp.concatenate([own[0, cy, cx, span, :], own[1, cy, cx, span, :]], axis=1)
                pair = dot(slices, rows, NT)
                panel[o, cy * 4 + cx] = pair[:16] + pair[16:]
            return carry

        lax.fori_loop(0, 4 * len(steps), chip, 0)

    for copy in core_copies:
        copy.wait_recv()
    panel_groups((0, 1, 2))
    for l in range(2):
        last[l].wait_recv()
        over_core(l, 3)
    for copy in core_copies[6:]:
        copy.wait_recv()
    panel_groups((3,))
    ay, ax = after // 4, lax.rem(after, 4)
    loads = [
        pltpu.make_async_copy(spread.at[:, :, :, :, pl.ds(CHUNK, 16)], gains, local_sem.at[1]),
        pltpu.make_async_copy(spread.at[:, y, x, :, pl.ds(0, CHUNK)], cand.at[0], local_sem.at[2]),
        pltpu.make_async_copy(spread.at[:, ay, ax, :, pl.ds(0, CHUNK)], cand.at[1], local_sem.at[3]),
    ]
    for load in loads:
        load.start()
    for load in loads:
        load.wait()

    def candidate(n, carry):
        which, slot = n // 4, n % 4
        span = pl.ds(pl.multiple_of(slot * T, T), T)
        for l in range(2):
            rows = jnp.concatenate([cand[which, 0, l, span, :], cand[which, 1, l, span, :]], axis=1)
            value = dot(sinv[l, 0], rows, NT) + dot(sinv[l, 1], rows, NT)
            weights[n, l, 0], weights[n, l, 1] = split(value)
        return carry

    lax.fori_loop(0, 8, candidate, 0)

    def chip_gains(at, carry):
        cy, cx = at // 4, at % 4
        for s in range(2):
            for l in range(2):
                parts = gains[s, cy, cx, l].astype(F32)
                for o in range(2):
                    gain = (parts[o : o + 1] + parts[2 + o : 3 + o]) + parts[4 + o : 5 + o]
                    reg[l, pl.ds((o * COLS + at) * 2 + s, 1), :] = gain
        return carry

    lax.fori_loop(0, COLS, chip_gains, 0)
    panel[0, 0] = upper[pl.ds(first, 16), pl.ds(pl.multiple_of(row * T, T), T)]

    passed = []
    for k in range(PARTS):
        part = pl.ds(k * ROWS, ROWS)
        for n, (source, target) in enumerate(((kn, knx), (oth, ox), (on, onx))):
            if n != 1 or k >= FORWARDED:
                bulk[k][n].wait_recv()
            passed.append(start(remote(source.at[part], target.at[part], pass_sem.at[n, k], across)))
    for k in range(PARTS):
        bulk[k][3].wait_recv()
    for copy in passed:
        copy.wait_recv()
    for copy in sent:
        copy.wait_send()

    @pl.when(jnp.logical_and(y == 0, x < 3))
    def _():
        lane_x.wait_send()

    @pl.when(y < 3)
    def _():
        lane_y.wait_send()


def exchange(tiles, regular, cmap):
    big = jax.ShapeDtypeStruct((HALF, CHUNK, T), BF16)
    spread = jax.ShapeDtypeStruct((2, 4, 4, 2, PACK, T), BF16)
    dma = pltpu.SemaphoreType.DMA
    anywhere, vmem = pl.BlockSpec(memory_space=pltpu.HBM), pl.BlockSpec(memory_space=pltpu.VMEM)
    return pl.pallas_call(
        exchange_kernel,
        name="exchange",
        out_shape=(big,) * 7 + (
            spread,
            jax.ShapeDtypeStruct((2, COLS, 16, T), F32),
            jax.ShapeDtypeStruct((8, 2, 2, N, T), BF16),
            jax.ShapeDtypeStruct((2, 64, T), F32),
        ),
        in_specs=[anywhere, vmem, vmem],
        out_specs=(anywhere,) * 8 + (vmem,) * 3,
        scratch_shapes=[
            pltpu.VMEM((PACK, T), BF16),
            pltpu.VMEM((CHUNK, T), BF16),
            pltpu.VMEM((CHUNK, T), F32),
            pltpu.VMEM((2, 2, N + 16, T), BF16),
            pltpu.VMEM((2, 4, 4, CHUNK, T), BF16),
            pltpu.VMEM((2, 2, 2, CHUNK, T), BF16),
            pltpu.VMEM((2, 4, 4, 2, 16, T), BF16),
            pltpu.VMEM((2, T, 2 * T), F32),
            pltpu.VMEM((2, N, N), F32),
            pltpu.VMEM((N, N), F32),
            pltpu.VMEM((2, N, N), BF16),
            pltpu.VMEM((2, 2, N, N), BF16),
            dma((5,)), dma((2,)), dma((3,)), dma((2,)), dma((4, 3, 2)), dma((2, 4, 2)), dma((4, PARTS, 2)), dma((3, PARTS, 2)),
        ],
        compiler_params=pltpu.CompilerParams(collective_id=0, has_side_effects=True, vmem_limit_bytes=56 << 20),
        cost_estimate=pl.CostEstimate(flops=4 * N**3, bytes_accessed=40 << 20, transcendentals=0),
    )(tiles, regular, cmap)


def place_of(q):
    return (q >> 1) & (COLS - 1), ((q >> 5) << 1) + (q & 1)


PAIR = 4


def parent_kernel(src, at, *refs):
    data, p_refs = refs[: 8 * PAIR], refs[8 * PAIR : 10 * PAIR]
    w_ref, reg_ref, out_ref, buf = refs[10 * PAIR :]
    row, col, half = at[0], at[1], at[3]
    diagonal = lax.broadcasted_iota(jnp.int32, (T, T), 0) == lax.broadcasted_iota(jnp.int32, (T, T), 1)
    from_rows, from_cols, spans, updates = {}, {}, {}, []
    for l in range(2):
        picks = []
        for j in range(4):
            from_col = src[l * 64 + ((j // 2) * COLS + col) * 2 + j % 2]
            chip, slot = place_of(from_col)
            far = jnp.where(chip == col, 0, 1)
            from_cols[l, j] = from_col
            spans[l, j] = pl.ds(far * CHUNK + slot, T, stride=4)
            picks.append(far * 4 + slot)
        rows = []
        for r in range(PAIR):
            from_row = src[l * 64 + 2 * (HALF * half + PAIR * pl.program_id(0) + r) + row]
            from_rows[l, r] = from_row
            mine = (from_row & 1) == row
            part = data[8 * r + 4 * l : 8 * r + 4 * l + 4]

            @pl.when(mine)
            def _():
                buf[l, r, :CHUNK] = part[0][0].astype(F32)
                buf[l, r, CHUNK:] = part[1][0].astype(F32)

            @pl.when(jnp.logical_not(mine))
            def _():
                buf[l, r, :CHUNK] = part[2][0].astype(F32)
                buf[l, r, CHUNK:] = part[3][0].astype(F32)

            p_ref = p_refs[2 * r + l]
            rows.append(jnp.concatenate([p_ref[0, 0, 0], p_ref[1, 0, 0]], axis=1))
            for j in range(4):

                @pl.when(from_row == from_cols[l, j])
                def _():
                    gain = reg_ref[l, pl.ds(from_row, 1), :]
                    buf[l, r, spans[l, j], :] = buf[l, r, spans[l, j], :] + jnp.where(diagonal, gain, 0.0)

        rows = jnp.concatenate(rows, axis=0)
        high = jnp.concatenate([w_ref[pick, l, 0] for pick in picks], axis=1)
        low = jnp.concatenate([w_ref[pick, l, 1] for pick in picks], axis=1)
        updates.append(dot(rows, high, NN) + dot(rows, low, NN))
    for r in range(PAIR):
        for j in range(4):
            total = None
            for l in range(2):
                value = buf[l, r, spans[l, j], :] - updates[l][r * T : (r + 1) * T, j * T : (j + 1) * T]
                value = value.astype(BF16).astype(F32)
                value = jnp.where(jnp.logical_and(from_rows[l, r] > 0, from_cols[l, j] > 0), value, 0.0)
                total = value if total is None else total + value
            out_ref[r, pl.ds(j, T, stride=4), :] = total


def parent_out(src, at, data, gathered, weights, reg):
    def source(i, r, l, src, at):
        return src[l * 64 + 2 * (HALF * at[3] + PAIR * i + r) + at[0]]

    def chunk_spec(r, l, partner, following):
        def index(i, src, at):
            q = source(i, r, l, src, at)
            wanted = (q & 1) == (at[0] ^ int(partner))
            less = 0 if l == 0 and not partner and not following else at[2]
            return (jnp.where(wanted, jnp.maximum((q >> 1) - less, 0), 0), 0, 0)

        return pl.BlockSpec((1, CHUNK, T), index)

    def p_spec(r, l):
        def index(i, src, at):
            chip, slot = place_of(source(i, r, l, src, at))
            return (0, chip, l, slot, 0)

        return pl.BlockSpec((2, 1, 1, T, T), index)

    pairs = [(r, l) for r in range(PAIR) for l in range(2)]
    return pl.pallas_call(
        parent_kernel,
        name="parent_out",
        out_shape=jax.ShapeDtypeStruct((HALF, CHUNK, T), F32),
        grid_spec=pltpu.PrefetchScalarGridSpec(
            num_scalar_prefetch=2,
            grid=(HALF // PAIR,),
            in_specs=[chunk_spec(r, l, p, f) for r, l in pairs for p in (False, True) for f in (False, True)]
            + [p_spec(r, l) for r, l in pairs]
            + [
                pl.BlockSpec((8, 2, 2, N, T), lambda i, src, at: (0, 0, 0, 0, 0)),
                pl.BlockSpec((2, 64, T), lambda i, src, at: (0, 0, 0)),
            ],
            out_specs=pl.BlockSpec((PAIR, CHUNK, T), lambda i, src, at: (i, 0, 0)),
            scratch_shapes=[pltpu.VMEM((2, PAIR, 2 * CHUNK, T), F32)],
        ),
        compiler_params=pltpu.CompilerParams(vmem_limit_bytes=56 << 20),
        cost_estimate=pl.CostEstimate(flops=2 * 2 * 4096 * N * CHUNK, bytes_accessed=14 << 20, transcendentals=0),
    )(src, at, *(data * PAIR), *([gathered] * (2 * PAIR)), weights, reg)


def shards(front_tiles, regular, child_map):
    row, col = lax.axis_index("row"), lax.axis_index("col")
    half = lax.axis_index("leaf") % 2
    base = jnp.where(half == 0, 1, HALF)
    tiles = front_tiles.reshape(2 * COLS, CHUNK, T)

    cmap = jnp.pad(child_map, ((0, 0), (0, T - child_map.shape[1])), constant_values=-1)
    kn, oth, on, kx, knx, ox, onx, spread, panel, weights, reg = exchange(tiles, regular.reshape(2, T), cmap)
    gathered = spread.reshape(2, COLS, 2, PACK, T)
    data = [tiles, kn, kx, knx, oth, on, ox, onx]
    src = gathered[0, 0, :, CHUNK + 6, :64].astype(jnp.int32).reshape(-1)
    at = jnp.stack([row, col, base, half]).astype(jnp.int32)

    panel = panel.transpose(0, 1, 3, 2).reshape(1, 2, COLS, 1, T, 16)
    parent = parent_out(src, at, data, gathered, weights, reg)
    return panel, parent.reshape(1, 1, COLS, 1, T, 2, 1, 2, T)


def solution(mesh):
    return jax.shard_map(
        shards,
        mesh=mesh,
        in_specs=(
            P("leaf", None, None, "row", None, None, "col", None, None),
            P("leaf", None, "col", "row", None),
            P("leaf", None),
        ),
        out_specs=(
            P("leaf", None, None, "row", None, "col"),
            P("leaf", None, None, "row", None, None, "col", None, None),
        ),
        check_vma=False,
    )
```
